128 devices in a mesh: section: 4 (over z_hi, core), ep: 32 (over y, x, z_lo).
Axes of the slice: x: 4, y: 4, z: 4 (z_hi: 2, z_lo: 2; z = z_hi * 2 + z_lo), core: 2. Of those that a mesh axis runs over, the one named last changes fastest.
Arguments:
- states: bfloat16 [4, 4096, 6144], P('section', 'ep'), may hold values from -6 to 6
- expert_ids: int32 [4, 4096, 2], P('section', 'ep'), may hold values from 0 to 7, all different within a row; in each aligned block of 128 rows (0 to 127, 128 to 255, ..., all dimensions but the last counted through in order) at most 48 rows name the same one
- gate_values: float32 [4, 4096, 2], P('section', 'ep'), may hold values from 0.1 to 1
- keep_mask: int32 [4, 4096, 2], P('section', 'ep'), may hold values 0 or 1
- w_gate: bfloat16 [4, 6144, 16384], P('section', None, 'ep'), may hold values from -0.078125 to 0.078125
- w_up: bfloat16 [4, 6144, 16384], P('section', None, 'ep'), may hold values from -0.078125 to 0.078125
- w_down: bfloat16 [4, 16384, 6144], P('section', 'ep'), may hold values from -0.0625 to 0.0625
Outputs:
- next_states: bfloat16 [4, 4096, 6144], P('section', 'ep')
The draws below stay inside these ranges and needn't reach their ends.
Inputs may be any that keep to these rules, and one draw needn't show every extreme that they name: `expert_ids`: in every section and every aligned block of 128 tokens (the rows of one index of ep), no expert is named by more than 48 tokens, a bound that some block reaches; the 2 experts of a token differ.
All inputs are finite; a program needn't handle non-finite values. No bound on the sum of `keep_mask` on one device may be relied on, other than what follows from the above.
Results may differ from the reference program's by a relative error of at most 0.0057.
Values may be sent and summed in bfloat16 or wider, within the bound.
No kernel may reach another device: no remote copies, remote signals or barrier semaphores. Data moves between devices by JAX's collectives and lax.ppermute only.
A program may use at most 128 MiB of HBM per device.

```python
import math
import jax
import jax.numpy as jnp
import numpy as np
from jax import lax

D = 6144
EXPERTS = 8
TOPK = 2
FF = 8192
EXP_WIN = 2
TOK_DEV = 128
CAP = 48
SECTIONS = 4
SLICES = 16
FFD = 512
TOKENS = 4096
N_EP = 32


def plant(values, stream_key, least, largest):
    shape = values.shape
    place = [jax.random.randint(jax.random.fold_in(stream_key, axis), (), 0, shape[axis]) for axis in range(len(shape))]
    values = values.at[tuple(place)].set(least)
    longest = shape.index(max(shape))
    place[longest] = (place[longest] + 1) % shape[longest]
    return values.at[tuple(place)].set(largest)


def block_scale(stream_key, shape, pieces, least, top_value):
    level, own = 1.0, jax.random.fold_in(stream_key, 6)
    for axis_at, blocks in pieces:
        steps = jnp.exp(jax.random.uniform(jax.random.fold_in(own, axis_at), (blocks,), jnp.float32, least / len(pieces), top_value / len(pieces)))
        level = level * jnp.repeat(steps, shape[axis_at] // blocks).reshape([-1 if axis == axis_at else 1 for axis in range(len(shape))])
    return level


def deal_out(key, own, number, rows, count, top, reach, lean):
    order = jax.random.permutation(key, count)
    packed, usual = load_shares(count, rows * top, reach, lean, True), load_shares(count, rows * top, reach, lean, False)
    places = jnp.arange(count)

    def named(lengths, offset_by):
        used = int((lengths > 0).sum())
        fixed = max(1, used // 4)
        passed = fixed + (places - fixed + offset_by * (used - fixed)) % max(1, count - fixed)
        return jnp.zeros((count,), jnp.int32).at[order[jnp.where(places < fixed, places, passed)]].set(jnp.asarray(lengths, jnp.int32))

    lengths = jnp.where(number % 4 == 0, named(packed, number // 4), named(usual, number - number // 4 - 1))
    mixed = jax.random.permutation(jax.random.fold_in(own, 3), count)
    source_of, sink = mixed[0:count // 2 * 2:2], mixed[1:count // 2 * 2:2]
    margin = jnp.minimum(lengths[source_of] - 1, reach - lengths[sink]) // 2
    margin = jnp.where((source_of == order[0]) | (sink == order[0]) | (lengths[sink] == 0), 0, jnp.maximum(margin, 0))
    passed = jax.random.randint(jax.random.fold_in(own, 4), (count // 2,), 0, 1 << 20) % (margin + 1)
    lengths = lengths.at[source_of].add(-passed).at[sink].add(passed)
    members = jnp.searchsorted(jnp.cumsum(lengths), jnp.arange(rows * top), side="right").astype(jnp.int32)
    table = members.reshape(top, rows).T
    table = table[jax.random.permutation(jax.random.fold_in(own, 1), rows)]
    offset_by = jax.random.randint(jax.random.fold_in(own, 2), (rows, 1), 0, top)
    return jnp.take_along_axis(table, (jnp.arange(top)[None, :] + offset_by) % top, axis=1)


def load_shares(count, total, reach, lean, full):
    weights = [(1 << 20) // math.isqrt(rank ** lean) + 1 for rank in range(1, count + 1)]
    largest = reach if full else min(reach, max(-(-total // count), total * weights[0] // sum(weights)))
    least = 1 if total - largest >= count - 1 else 0
    counts, spare = [largest] + [least] * (count - 1), total - largest - least * (count - 1)
    while spare > 0:
        candidates = [i for i in range(1, count) if counts[i] < largest] or [i for i in range(1, count) if counts[i] < reach]
        whole, budget = sum([weights[i] for i in candidates]), spare
        for i in candidates:
            extra = min(reach - counts[i], max(1, budget * weights[i] // whole), spare)
            counts[i] = counts[i] + extra
            spare = spare - extra
    return np.array(counts)


def scatter_about(stream_key, shape, spread, limit, split=(), kind=jnp.bfloat16):
    entries = spread * jax.random.normal(stream_key, shape, jnp.float32)
    if split:
        entries = entries * block_scale(stream_key, shape, split, -0.22, 0.18)
    return jnp.clip(entries, -limit, limit).astype(kind)


def setup_inputs(seed: int = 0) -> dict:
    streams_of = jax.random.split(jax.random.key(seed), 8)
    states = scatter_about(streams_of[0], (SECTIONS, TOKENS, D), 1.0, 6.0, ((0, 4), (1, 32)))
    expert_ids_keys = jax.random.split(jax.random.fold_in(streams_of[1], 1), SECTIONS * TOKENS // TOK_DEV)
    expert_ids_turns = jax.random.permutation(jax.random.fold_in(streams_of[1], 3), SECTIONS * TOKENS // TOK_DEV)
    expert_ids = jax.vmap(lambda own, number: deal_out(jax.random.fold_in(streams_of[1], 2), own, number, TOK_DEV, EXPERTS, TOPK, CAP, 2))(expert_ids_keys, expert_ids_turns).reshape((SECTIONS, TOKENS, TOPK))
    gate_values = jnp.clip(0.1 + 0.9 * jax.random.uniform(streams_of[2], (SECTIONS, TOKENS, TOPK), jnp.float32) ** block_scale(streams_of[2], (SECTIONS, TOKENS, TOPK), ((0, 4), (1, 32)), -0.2, 0.2), 0.1, 1.0)
    keep_mask = plant((jax.random.randint(streams_of[3], (SECTIONS, TOKENS, TOPK), 0, 8) < 7).astype(jnp.int32), jax.random.fold_in(streams_of[3], 1), 0, 1)
    w_gate = scatter_about(streams_of[4], (SECTIONS, D, EXP_WIN * FF), D ** -0.5, 0.078125, ((0, 4), (2, 32)))
    w_up = scatter_about(streams_of[5], (SECTIONS, D, EXP_WIN * FF), D ** -0.5, 0.078125, ((0, 4), (2, 32)))
    w_down = scatter_about(streams_of[6], (SECTIONS, EXP_WIN * FF, D), FF ** -0.5, 0.0625, ((0, 4), (1, 32)))
    return {"states": states, "expert_ids": expert_ids, "gate_values": gate_values, "keep_mask": keep_mask, "w_gate": w_gate, "w_up": w_up, "w_down": w_down}


def expert_apply(rows_sel, gate_e, up_e, down_e):
    gate_proj = jnp.dot(rows_sel, gate_e, preferred_element_type=jnp.float32)
    up_proj = jnp.dot(rows_sel, up_e, preferred_element_type=jnp.float32)
    hidden = (jax.nn.silu(gate_proj) * up_proj).astype(jnp.bfloat16)

    def add_slice(total, index):
        part_hidden = lax.dynamic_slice_in_dim(hidden, (index * FFD).astype(jnp.int32), FFD, 1)
        part_weight = lax.dynamic_slice_in_dim(down_e, (index * FFD).astype(jnp.int32), FFD, 0)
        term = jnp.dot(part_hidden, part_weight, preferred_element_type=jnp.float32).astype(jnp.bfloat16)
        term = lax.optimization_barrier(term)
        return total + term.astype(jnp.float32), None

    start_total = jnp.zeros((rows_sel.shape[0], down_e.shape[1]), jnp.float32)
    total, unused = lax.scan(add_slice, start_total, jnp.arange(SLICES, dtype=jnp.int32))
    return total


def reference(states, expert_ids, gate_values, keep_mask, w_gate, w_up, w_down):
    results = []
    for section in range(SECTIONS):
        tokens_all = states[section]
        mixed = jnp.zeros((TOKENS, D), jnp.float32)
        for expert in range(EXP_WIN):
            chosen = (expert_ids[section] == expert) & (keep_mask[section] == 1)
            picked = jnp.any(chosen, axis=1)
            weight_tok = jnp.sum(jnp.where(chosen, gate_values[section], jnp.zeros_like(gate_values[section])), axis=1)
            index_list = jnp.nonzero(picked, size=N_EP * CAP, fill_value=0)[0].astype(jnp.int32)
            valid = jnp.arange(N_EP * CAP, dtype=jnp.int32) < jnp.sum(picked.astype(jnp.int32))
            rows_sel = tokens_all[index_list]
            result = expert_apply(rows_sel,
                                  w_gate[section][:, expert * FF:(expert + 1) * FF],
                                  w_up[section][:, expert * FF:(expert + 1) * FF],
                                  w_down[section][expert * FF:(expert + 1) * FF, :])
            scale = jnp.where(valid, weight_tok[index_list], jnp.zeros_like(weight_tok[index_list]))
            mixed = mixed.at[index_list].add(scale[:, None] * result)
        results.append(mixed.astype(jnp.bfloat16))
    return jnp.roll(jnp.stack(results), 1, axis=0)
```

```python
import jax
import jax.numpy as jnp
from jax import lax
from jax.sharding import Mesh, PartitionSpec as P

EXP_WIN = 2
CAP = 48
PIECE = 24
F32 = jnp.float32
BF16 = jnp.bfloat16


def shift(value, axis, by):
    n = lax.axis_size(axis)
    return lax.ppermute(value, axis, [(i, (i + by) % n) for i in range(n)])


def to_partner(value):
    return lax.ppermute(value, ("yh", "yl"), [(y, 3 - y) for y in range(4)])


def to_next_section(value):
    return lax.ppermute(value, ("zh", "core"), [(s, (s + 1) % 4) for s in range(4)])


def to_next_section_partner(value):
    pairs = [(s * 4 + y, (s + 1) % 4 * 4 + 3 - y) for s in range(4) for y in range(4)]
    return lax.ppermute(value, ("zh", "core", "yh", "yl"), pairs)


def add(*terms):
    total = terms[0].astype(F32)
    for term in terms[1:]:
        total = total + term.astype(F32)
    return total.astype(BF16)


def split(rows, sizes):
    out, start = [], 0
    for size in sizes:
        out.append(rows[start : start + size])
        start += size
    return out


def spread_across(piece, first, second):
    near = jnp.concatenate([piece, shift(piece, first, 1)])
    far = shift(near, second, 1)
    near_left, near_right = shift(near, "x", 1), shift(near, "x", -1)
    far_left, far_right = shift(far, "x", 1), shift(far, "x", -1)
    near_opposite = shift(near_left, "x", 1)
    far_opposite = shift(far_right, "x", -1)
    return [near, far, near_left, near_right, far_left, far_right, near_opposite, far_opposite]


def reduce_across(parts, first, second):
    near, far, near_left, near_right, far_left, far_right, near_opposite, far_opposite = parts
    near_right_sent = shift(near_right, "x", 1)
    far_left_sent = shift(far_left, "x", -1)
    near_left = add(near_left, shift(near_opposite, "x", -1))
    far_right = add(far_right, shift(far_opposite, "x", 1))
    near_left_sent = shift(near_left, "x", -1)
    far_right_sent = shift(far_right, "x", 1)
    far = add(far, far_left_sent, far_right_sent)
    far_sent = shift(far, second, 1)
    near = add(near, near_left_sent, near_right_sent, far_sent)
    half = near.shape[0] // 2
    return add(near[:half], shift(near[half:], first, 1))


def spread_along(piece, way, first, second):
    behind, ahead = shift(piece, "x", way), shift(piece, "x", -way)
    opposite = shift(behind, "x", way)
    ring = jnp.concatenate([piece, behind, ahead, opposite])
    across = shift(ring, first, 1)
    return [ring, across, shift(ring, second, 1), shift(across, second, 1)]


def reduce_along(parts, way, first, second):
    ring, across, ring_second, across_second = parts
    ring_sent = shift(ring_second, second, 1)
    across = add(across, shift(across_second, second, 1))
    ring = add(ring, ring_sent, shift(across, first, 1))
    size = ring.shape[0] // 4
    piece, behind, ahead, opposite = split(ring, [size] * 4)
    ahead_sent = shift(ahead, "x", way)
    behind = add(behind, shift(opposite, "x", -way))
    return add(piece, ahead_sent, shift(behind, "x", -way))


def experts(pieces, gate_matrix, up_matrix, down_matrix):
    rows = jnp.concatenate(pieces)
    gate = jnp.dot(rows, gate_matrix, preferred_element_type=F32)
    up = jnp.dot(rows, up_matrix, preferred_element_type=F32)
    hidden = (jax.nn.silu(gate) * up).astype(BF16)
    out = jnp.dot(hidden, down_matrix, preferred_element_type=F32).astype(BF16)
    return split(out, [p.shape[0] for p in pieces])


def slots(ids, keep, expert):
    chosen = (ids == expert) & (keep == 1)
    picked = jnp.any(chosen, axis=1)
    position = jnp.cumsum(picked.astype(jnp.int32)) - 1
    return chosen, picked, position


def body(states, expert_ids, gate_values, keep_mask, w_gate, w_up, w_down):
    tokens = states[0]
    ids, gates, keep = expert_ids[0], gate_values[0], keep_mask[0]
    matrices = (w_gate[0], w_up[0], w_down[0])
    mine = lax.axis_index("yh")
    other = 1 - mine

    def compact(expert):
        _, picked, position = slots(ids, keep, expert)
        table = (position[None] == jnp.arange(CAP, dtype=jnp.int32)[:, None]) & picked[None]
        return jnp.dot(table.astype(BF16), tokens, preferred_element_type=F32).astype(BF16)

    partner_rows = to_partner(compact(other))
    own_rows = compact(mine)

    own_a, own_b = split(own_rows, [PIECE] * 2)
    partner_a, partner_b = split(partner_rows, [PIECE] * 2)

    b_parts = spread_along(own_b, 1, "zl", "yl")
    a_parts = spread_across(own_a, "yl", "zl")
    d_parts = spread_along(partner_b, -1, "yl", "zl")
    c_parts = spread_across(partner_a, "zl", "yl")

    a_out = experts(a_parts, *matrices)
    bd_out = experts(b_parts[:2] + d_parts[:2], *matrices)
    b2d2_out = experts(b_parts[2:] + d_parts[2:], *matrices)
    c_out = experts(c_parts, *matrices)

    a_sum = reduce_across(a_out, "yl", "zl")
    c_sum = reduce_across(c_out, "zl", "yl")
    b_sum = reduce_along(bd_out[:2] + b2d2_out[:2], 1, "zl", "yl")
    d_sum = reduce_along(bd_out[2:] + b2d2_out[2:], -1, "yl", "zl")

    own_done = jnp.concatenate([to_next_section(a_sum), to_next_section(b_sum)])
    other_done = jnp.concatenate(
        [to_next_section_partner(c_sum), to_next_section_partner(d_sum)]
    )

    ids, gates, keep = (to_next_section(v) for v in (ids, gates, keep))

    def contribution(expert, done):
        chosen, picked, position = slots(ids, keep, expert)
        weight = jnp.sum(jnp.where(chosen, gates, 0.0), axis=1)
        table = (position[:, None] == jnp.arange(CAP, dtype=jnp.int32)[None]) & picked[:, None]
        rows = jnp.dot(table.astype(BF16), done, preferred_element_type=F32)
        return weight[:, None] * rows

    mixed = contribution(mine, own_done) + contribution(other, other_done)
    return mixed.astype(BF16)[None]


def solution(mesh):
    shape = (2, 2, 2, 2, 4, 2)
    fine = Mesh(mesh.devices.reshape(shape), ("zh", "core", "yh", "yl", "x", "zl"))
    section, ep = ("zh", "core"), ("yh", "yl", "x", "zl")
    rows = P(section, ep, None)
    columns = P(section, None, ep)
    return jax.shard_map(
        body,
        mesh=fine,
        in_specs=(rows, rows, rows, rows, columns, columns, rows),
        out_specs=rows,
        check_vma=False,
    )
```

```python
import jax
import jax.numpy as jnp
from jax import lax
from jax.sharding import Mesh, PartitionSpec as P

CAP = 48
PIECE = 24
F32 = jnp.float32
BF16 = jnp.bfloat16


def shift(value, axis, by):
    n = lax.axis_size(axis)
    return lax.ppermute(value, axis, [(i, (i + by) % n) for i in range(n)])


def right(value):
    return shift(value, "x", 1)


def left(value):
    return shift(value, "x", -1)


def over_y(value):
    return shift(value, "yl", 1)


def over_z(value):
    return shift(value, "zl", 1)


def to_partner(value):
    return lax.ppermute(value, ("yh", "yl"), [(y, 3 - y) for y in range(4)])


def to_next_section(value):
    return lax.ppermute(value, ("zh", "core"), [(s, (s + 1) % 4) for s in range(4)])


def to_next_section_partner(value):
    pairs = [(s * 4 + y, (s + 1) % 4 * 4 + 3 - y) for s in range(4) for y in range(4)]
    return lax.ppermute(value, ("zh", "core", "yh", "yl"), pairs)


def together(*values):
    return lax.optimization_barrier(values)


def join(*pieces):
    return jnp.concatenate(pieces)


def add(*terms):
    total = terms[0].astype(F32)
    for term in terms[1:]:
        total = total + term.astype(F32)
    return total.astype(BF16)


def split(rows, count):
    size = rows.shape[0] // count
    return [rows[i * size : (i + 1) * size] for i in range(count)]


def experts(pieces, gate_matrix, up_matrix, down_matrix):
    rows = jnp.concatenate(pieces)
    gate = jnp.dot(rows, gate_matrix, preferred_element_type=F32)
    up = jnp.dot(rows, up_matrix, preferred_element_type=F32)
    hidden = (jax.nn.silu(gate) * up).astype(BF16)
    out = jnp.dot(hidden, down_matrix, preferred_element_type=F32).astype(BF16)
    return split(out, len(pieces))


def slots(ids, keep, expert):
    chosen = (ids == expert) & (keep == 1)
    picked = jnp.any(chosen, axis=1)
    position = jnp.cumsum(picked.astype(jnp.int32)) - 1
    return chosen, picked, position


def body(states, expert_ids, gate_values, keep_mask, w_gate, w_up, w_down):
    tokens = states[0]
    ids, gates, keep = expert_ids[0], gate_values[0], keep_mask[0]
    matrices = (w_gate[0], w_up[0], w_down[0])
    mine = lax.axis_index("yh")
    other = 1 - mine

    def compact(expert):
        _, picked, position = slots(ids, keep, expert)
        table = (position[None] == jnp.arange(CAP, dtype=jnp.int32)[:, None]) & picked[None]
        return jnp.dot(table.astype(BF16), tokens, preferred_element_type=F32).astype(BF16)

    partner = to_partner(compact(other))
    own = compact(mine)
    next_ids, next_gates, next_keep = (to_next_section(v) for v in (ids, gates, keep))
    own, partner, ids, gates, keep = together(own, partner, next_ids, next_gates, next_keep)
    (a1, b), (a2, g) = split(own, 2), split(partner, 2)

    b_behind, g_behind, a1_y, a2_z = together(right(b), left(g), over_y(a1), over_z(a2))
    a1_near, a2_near = join(a1, a1_y), join(a2, a2_z)
    from_left, from_right, a1_far, a2_far = together(
        right(join(b_behind, g)), left(join(g_behind, b)), over_z(a1_near), over_y(a2_near)
    )
    b_opposite, g_ahead = split(from_left, 2)
    g_opposite, b_ahead = split(from_right, 2)
    near, far = join(a1_near, a2_near), join(a1_far, a2_far)
    b_ring = join(b, b_behind, b_ahead, b_opposite)
    g_ring = join(g, g_behind, g_ahead, g_opposite)

    near, far, b_ring, g_ring = together(near, far, b_ring, g_ring)
    near_left, far_right, g_y, b_z = right(near), left(far), over_y(g_ring), over_z(b_ring)
    out0 = experts([near, far, b_ring, g_ring], *matrices)
    near_left, far_right, g_y, b_z, b_ring, g_ring, *out0 = together(
        near_left, far_right, g_y, b_z, b_ring, g_ring, *out0
    )

    near_opposite, far_opposite, b_y, g_z = (
        right(near_left), left(far_right), over_y(b_ring), over_z(g_ring)
    )
    out1 = experts([near_left, far_right, g_y, b_z], *matrices)
    near_opposite, far_opposite, b_y, g_z, near, far, b_z, g_y, *out1 = together(
        near_opposite, far_opposite, b_y, g_z, near, far, b_z, g_y, *out1
    )

    near_right, far_left, b_yz, g_zy = left(near), right(far), over_y(b_z), over_z(g_y)
    out2 = experts([near_opposite, far_opposite, b_y, g_z], *matrices)
    near_right, far_left, b_yz, g_zy, *out2 = together(near_right, far_left, b_yz, g_zy, *out2)

    near, far, b_ring, g_ring = out0
    near_left, far_right, g_y, b_z = out1
    near_opposite, far_opposite, b_y, g_z = out2
    got = left(near_opposite), right(far_opposite), over_y(b_y), over_z(g_z)
    out3 = experts([near_right, far_left, b_yz, g_zy], *matrices)
    *got, near_right, far_left, b_yz, g_zy = together(*got, *out3)
    near_left, far_right = add(near_left, got[0]), add(far_right, got[1])
    b_back, g_back = got[2:]

    got = together(left(near_left), right(far_right), over_y(b_yz), over_z(g_zy))
    near_back, far_back = got[:2]
    b_z, g_y = add(b_z, got[2]), add(g_y, got[3])

    got = together(right(near_right), left(far_left), over_y(g_y), over_z(b_z))
    near, far = add(near, near_back, got[0]), add(far, far_back, got[1])
    g_ring, b_ring = add(g_ring, g_back, got[2]), add(b_ring, b_back, got[3])

    (a1_near, a2_near), (a1_far, a2_far) = split(near, 2), split(far, 2)
    b, b_behind, b_ahead, b_opposite = split(b_ring, 4)
    g, g_behind, g_ahead, g_opposite = split(g_ring, 4)
    got = together(
        left(join(b_opposite, g_ahead)), right(join(g_opposite, b_ahead)), over_z(a1_far), over_y(a2_far)
    )
    (b_behind_back, g_back), (g_behind_back, b_back) = split(got[0], 2), split(got[1], 2)
    a1_near, a2_near = add(a1_near, got[2]), add(a2_near, got[3])
    (a1, a1_y), (a2, a2_z) = split(a1_near, 2), split(a2_near, 2)
    got = together(
        left(add(b_behind, b_behind_back)), right(add(g_behind, g_behind_back)), over_y(a1_y), over_z(a2_z)
    )
    own = join(add(a1, got[2]), add(b, b_back, got[0]))
    partner = join(add(a2, got[3]), add(g, g_back, got[1]))

    own_done, other_done = to_next_section(own), to_next_section_partner(partner)

    def contribution(expert, done):
        chosen, picked, position = slots(ids, keep, expert)
        weight = jnp.sum(jnp.where(chosen, gates, 0.0), axis=1)
        table = (position[:, None] == jnp.arange(CAP, dtype=jnp.int32)[None]) & picked[:, None]
        rows = jnp.dot(table.astype(BF16), done, preferred_element_type=F32)
        return weight[:, None] * rows

    mixed = contribution(mine, own_done) + contribution(other, other_done)
    return mixed.astype(BF16)[None]


def solution(mesh):
    shape = (2, 2, 2, 2, 4, 2)
    fine = Mesh(mesh.devices.reshape(shape), ("zh", "core", "yh", "yl", "x", "zl"))
    section, ep = ("zh", "core"), ("yh", "yl", "x", "zl")
    rows = P(section, ep, None)
    columns = P(section, None, ep)
    return jax.shard_map(
        body,
        mesh=fine,
        in_specs=(rows, rows, rows, rows, columns, columns, rows),
        out_specs=rows,
        check_vma=False,
    )
```

```python
import jax
import jax.numpy as jnp
from jax import lax
from jax.experimental import pallas as pl
from jax.experimental.pallas import tpu as pltpu
from jax.sharding import Mesh, PartitionSpec as P

CAP = 48
PIECE = 24
F32 = jnp.float32
BF16 = jnp.bfloat16


def shift(value, axis, by):
    n = lax.axis_size(axis)
    return lax.ppermute(value, axis, [(i, (i + by) % n) for i in range(n)])


def right(value):
    return shift(value, "x", 1)


def left(value):
    return shift(value, "x", -1)


def over_y(value):
    return shift(value, "yl", 1)


def over_z(value):
    return shift(value, "zl", 1)


def to_partner(value):
    return lax.ppermute(value, ("yh", "yl"), [(y, 3 - y) for y in range(4)])


def to_next_section(value):
    return lax.ppermute(value, ("zh", "core"), [(s, (s + 1) % 4) for s in range(4)])


def to_next_section_partner(value):
    pairs = [(s * 4 + y, (s + 1) % 4 * 4 + 3 - y) for s in range(4) for y in range(4)]
    return lax.ppermute(value, ("zh", "core", "yh", "yl"), pairs)


def together(*values):
    return lax.optimization_barrier(values)


def join(*pieces):
    return jnp.concatenate(pieces)


def add(*terms):
    total = terms[0].astype(F32)
    for term in terms[1:]:
        total = total + term.astype(F32)
    return total.astype(BF16)


def split(rows, count):
    size = rows.shape[0] // count
    return [rows[i * size : (i + 1) * size] for i in range(count)]


TILE = 1536


def experts_kernel(*refs):
    rows, (w_gate, w_up, w_down), rest = refs[:4], refs[4:7], refs[7:]
    outs, (gate, up, hidden) = rest[:4], rest[4:]
    step = pl.program_id(0)
    half = pl.num_programs(0) // 2

    @pl.when(step < half)
    def _():
        block = jnp.concatenate([r[...] for r in rows])
        gate_part = jnp.dot(block, w_gate[...], preferred_element_type=F32)
        up_part = jnp.dot(block, w_up[...], preferred_element_type=F32)

        @pl.when(step == 0)
        def _():
            gate[...] = gate_part
            up[...] = up_part

        @pl.when(step > 0)
        def _():
            gate[...] += gate_part
            up[...] += up_part

    @pl.when(step >= half)
    def _():
        @pl.when(step == half)
        def _():
            v = gate[...]
            hidden[...] = (v / (1.0 + jnp.exp(-v)) * up[...]).astype(BF16)

        out = jnp.dot(hidden[...], w_down[...], preferred_element_type=F32).astype(BF16)
        size = outs[0].shape[0]
        for i, o in enumerate(outs):
            o[...] = out[i * size : (i + 1) * size]


def experts(pieces, gate_matrix, up_matrix, down_matrix):
    size, width = pieces[0].shape
    units = gate_matrix.shape[1]
    half = width // TILE
    first = lambda i: jnp.minimum(i, half - 1)
    second = lambda i: jnp.maximum(i - half, 0)
    rows_in = pl.BlockSpec((size, TILE), lambda i: (0, first(i)))
    rows_out = pl.BlockSpec((size, TILE), lambda i: (0, second(i)))
    into = pl.BlockSpec((TILE, units), lambda i: (first(i), 0))
    out_of = pl.BlockSpec((units, TILE), lambda i: (0, second(i)))
    total = len(pieces) * size
    return pl.pallas_call(
        experts_kernel,
        grid=(2 * half,),
        in_specs=[rows_in] * 4 + [into, into, out_of],
        out_specs=[rows_out] * 4,
        out_shape=[jax.ShapeDtypeStruct((size, width), BF16)] * 4,
        scratch_shapes=[
            pltpu.VMEM((total, units), F32),
            pltpu.VMEM((total, units), F32),
            pltpu.VMEM((total, units), BF16),
        ],
        compiler_params=pltpu.CompilerParams(
            dimension_semantics=("arbitrary",), vmem_limit_bytes=24 << 20
        ),
        cost_estimate=pl.CostEstimate(
            flops=6 * total * width * units,
            transcendentals=total * units,
            bytes_accessed=6 * width * units + 4 * total * width,
        ),
        name="experts",
    )(*pieces, gate_matrix, up_matrix, down_matrix)


def slots(ids, keep, expert):
    chosen = (ids == expert) & (keep == 1)
    picked = jnp.any(chosen, axis=1)
    position = jnp.cumsum(picked.astype(jnp.int32)) - 1
    return chosen, picked, position


def body(states, expert_ids, gate_values, keep_mask, w_gate, w_up, w_down):
    tokens = states[0]
    ids, gates, keep = expert_ids[0], gate_values[0], keep_mask[0]
    matrices = (w_gate[0], w_up[0], w_down[0])
    mine = lax.axis_index("yh")
    other = 1 - mine

    def compact(expert, tokens):
        _, picked, position = slots(ids, keep, expert)
        table = (position[None] == jnp.arange(CAP, dtype=jnp.int32)[:, None]) & picked[None]
        return jnp.dot(table.astype(BF16), tokens, preferred_element_type=F32).astype(BF16)

    others, tokens = together(compact(other, tokens), tokens)
    partner = to_partner(others)
    own = compact(mine, tokens)

    a1, b = split(own, 2)
    a1_y, b_behind, b_ahead = over_y(a1), right(b), left(b)
    a1_near = join(a1, a1_y)
    a1_far, b_opposite = over_z(a1_near), right(b_behind)
    b_ring = join(b, b_behind, b_ahead, b_opposite)

    a2, g = split(partner, 2)
    a2_z, g_behind, g_ahead = over_z(a2), left(g), right(g)
    b_y = over_y(b_ring)
    g_behind, g_ahead, b_ring_z = together(g_behind, g_ahead, b_ring)
    g_opposite = left(g_behind)
    a2_near = join(a2, a2_z)
    near = join(a1_near, a2_near)
    a2_far, b_z = over_y(a2_near), over_z(b_ring_z)
    near_late, g_opposite_done = together(near, g_opposite)
    near_left, near_right = right(near), left(near_late)
    g_ring = join(g, g_behind, g_ahead, g_opposite_done)

    b_y, g_ring_out = together(b_y, g_ring)
    g_y, g_z = over_y(g_ring_out), over_z(g_ring_out)
    far = join(a1_far, a2_far)
    near, b_ring, g_ring, b_y = experts([near, b_ring, g_ring, b_y], *matrices)
    far_left, far_right = right(far), left(far)

    near_left, near_right, far, b_z, near, b_ring, g_ring, b_y = together(
        near_left, near_right, far, b_z, near, b_ring, g_ring, b_y
    )
    near_opposite, b_yz = right(near_left), over_y(b_z)
    near_left, near_right, far, b_z = experts([near_left, near_right, far, b_z], *matrices)

    far_left, far_right, g_y, g_z, near_left, near_right, far, b_z = together(
        far_left, far_right, g_y, g_z, near_left, near_right, far, b_z
    )
    far_opposite, g_zy = left(far_right), over_z(g_y)
    far_left, far_right, g_y, g_z = experts([far_left, far_right, g_y, g_z], *matrices)

    near_opposite, far_opposite, b_yz, g_zy, far_left, far_right, g_y, g_z = together(
        near_opposite, far_opposite, b_yz, g_zy, far_left, far_right, g_y, g_z
    )
    near_back, far_back, b_back, g_back = (
        right(near_right), left(far_left), over_y(b_y), over_z(g_z)
    )
    near_opposite, far_opposite, b_yz, g_zy = experts(
        [near_opposite, far_opposite, b_yz, g_zy], *matrices
    )

    near_opposite, far_opposite, b_yz, g_zy, near_back, far_back, b_back, g_back = together(
        near_opposite, far_opposite, b_yz, g_zy, near_back, far_back, b_back, g_back
    )
    got = left(near_opposite), right(far_opposite), over_y(b_yz), over_z(g_zy)
    near_left, far_right = add(near_left, got[0]), add(far_right, got[1])
    b_z, g_y = add(b_z, got[2]), add(g_y, got[3])
    ids, gates, keep, near_left, far_right, b_z, g_y = together(
        ids, gates, keep, near_left, far_right, b_z, g_y
    )

    got = together(left(near_left), right(far_right), over_y(g_y), over_z(b_z))
    ids, gates, keep = (to_next_section(v) for v in (ids, gates, keep))
    near, far = add(near, near_back, got[0]), add(far, far_back, got[1])
    g_ring, b_ring = add(g_ring, g_back, got[2]), add(b_ring, b_back, got[3])

    (a1_near, a2_near), (a1_far, a2_far) = split(near, 2), split(far, 2)
    b, b_behind, b_ahead, b_opposite = split(b_ring, 4)
    g, g_behind, g_ahead, g_opposite = split(g_ring, 4)
    got = together(
        left(join(b_opposite, g_ahead)), right(join(g_opposite, b_ahead)), over_z(a1_far), over_y(a2_far)
    )
    (b_behind_back, g_back), (g_behind_back, b_back) = split(got[0], 2), split(got[1], 2)
    a1_near, a2_near = add(a1_near, got[2]), add(a2_near, got[3])
    (a1, a1_y), (a2, a2_z) = split(a1_near, 2), split(a2_near, 2)
    got = together(
        left(add(b_behind, b_behind_back)), right(add(g_behind, g_behind_back)), over_y(a1_y), over_z(a2_z)
    )
    own = join(add(a1, got[2]), add(b, b_back, got[0]))
    partner = join(add(a2, got[3]), add(g, g_back, got[1]))

    own_done, other_done = to_next_section(own), to_next_section_partner(partner)

    def contribution(expert, done):
        chosen, picked, position = slots(ids, keep, expert)
        weight = jnp.sum(jnp.where(chosen, gates, 0.0), axis=1)
        table = (position[:, None] == jnp.arange(CAP, dtype=jnp.int32)[None]) & picked[:, None]
        rows = jnp.dot(table.astype(BF16), done, preferred_element_type=F32)
        return weight[:, None] * rows

    mixed = contribution(mine, own_done) + contribution(other, other_done)
    return mixed.astype(BF16)[None]


def solution(mesh):
    shape = (2, 2, 2, 2, 4, 2)
    fine = Mesh(mesh.devices.reshape(shape), ("zh", "core", "yh", "yl", "x", "zl"))
    section, ep = ("zh", "core"), ("yh", "yl", "x", "zl")
    rows = P(section, ep, None)
    columns = P(section, None, ep)
    return jax.shard_map(
        body,
        mesh=fine,
        in_specs=(rows, rows, rows, rows, columns, columns, rows),
        out_specs=rows,
        check_vma=False,
    )
```

```python
import jax
import jax.numpy as jnp
from jax import lax
from jax.experimental import pallas as pl
from jax.experimental.pallas import tpu as pltpu
from jax.sharding import Mesh, PartitionSpec as P

CAP = 48
PIECE = 24
F32 = jnp.float32
BF16 = jnp.bfloat16


def shift(value, axis, by):
    n = lax.axis_size(axis)
    return lax.ppermute(value, axis, [(i, (i + by) % n) for i in range(n)])


def right(value):
    return shift(value, "x", 1)


def left(value):
    return shift(value, "x", -1)


def over_y(value):
    return shift(value, "yl", 1)


def over_z(value):
    return shift(value, "zl", 1)


def to_partner(value):
    return lax.ppermute(value, ("yh", "yl"), [(y, 3 - y) for y in range(4)])


def to_next_section(value):
    return lax.ppermute(value, ("zh", "core"), [(s, (s + 1) % 4) for s in range(4)])


def to_owner(value):
    pairs = [(s * 2 + z, (s + 1) % 4 * 2 + 1 - z) for s in range(4) for z in range(2)]
    return lax.ppermute(value, ("zh", "core", "zl"), pairs)


def to_owner_across(value):
    pairs = [
        ((s * 4 + y) * 2 + z, ((s + 1) % 4 * 4 + 3 - y) * 2 + 1 - z)
        for s in range(4)
        for y in range(4)
        for z in range(2)
    ]
    return lax.ppermute(value, ("zh", "core", "yh", "yl", "zl"), pairs)


def together(*values):
    return lax.optimization_barrier(values)


def join(*pieces):
    return jnp.concatenate(pieces)


def add(*terms):
    total = terms[0].astype(F32)
    for term in terms[1:]:
        total = total + term.astype(F32)
    return total.astype(BF16)


def split(rows, count):
    size = rows.shape[0] // count
    return [rows[i * size : (i + 1) * size] for i in range(count)]


TILE = 1536


def experts_kernel(*refs):
    count = (len(refs) - 6) // 2
    rows, (w_gate, w_up, w_down), rest = refs[:count], refs[count : count + 3], refs[count + 3 :]
    outs, (gate, up, hidden) = rest[:count], rest[count:]
    step = pl.program_id(0)
    half = pl.num_programs(0) // 2

    @pl.when(step < half)
    def _():
        block = jnp.concatenate([r[...] for r in rows])
        gate_part = jnp.dot(block, w_gate[...], preferred_element_type=F32)
        up_part = jnp.dot(block, w_up[...], preferred_element_type=F32)

        @pl.when(step == 0)
        def _():
            gate[...] = gate_part
            up[...] = up_part

        @pl.when(step > 0)
        def _():
            gate[...] += gate_part
            up[...] += up_part

    @pl.when(step >= half)
    def _():
        @pl.when(step == half)
        def _():
            v = gate[...]
            hidden[...] = (v / (1.0 + jnp.exp(-v)) * up[...]).astype(BF16)

        out = jnp.dot(hidden[...], w_down[...], preferred_element_type=F32).astype(BF16)
        start = 0
        for o in outs:
            o[...] = out[start : start + o.shape[0]]
            start += o.shape[0]


def experts(pieces, gate_matrix, up_matrix, down_matrix):
    sizes, width = [p.shape[0] for p in pieces], pieces[0].shape[1]
    units = gate_matrix.shape[1]
    half = width // TILE
    first = lambda i: jnp.minimum(i, half - 1)
    second = lambda i: jnp.maximum(i - half, 0)
    rows_in = [pl.BlockSpec((n, TILE), lambda i: (0, first(i))) for n in sizes]
    rows_out = [pl.BlockSpec((n, TILE), lambda i: (0, second(i))) for n in sizes]
    into = pl.BlockSpec((TILE, units), lambda i: (first(i), 0))
    out_of = pl.BlockSpec((units, TILE), lambda i: (0, second(i)))
    total = sum(sizes)
    return pl.pallas_call(
        experts_kernel,
        grid=(2 * half,),
        in_specs=rows_in + [into, into, out_of],
        out_specs=rows_out,
        out_shape=[jax.ShapeDtypeStruct((n, width), BF16) for n in sizes],
        scratch_shapes=[
            pltpu.VMEM((total, units), F32),
            pltpu.VMEM((total, units), F32),
            pltpu.VMEM((total, units), BF16),
        ],
        compiler_params=pltpu.CompilerParams(
            dimension_semantics=("arbitrary",), vmem_limit_bytes=24 << 20
        ),
        cost_estimate=pl.CostEstimate(
            flops=6 * total * width * units,
            transcendentals=total * units,
            bytes_accessed=6 * width * units + 4 * total * width,
        ),
        name="experts",
    )(*pieces, gate_matrix, up_matrix, down_matrix)


def slots(ids, keep, expert):
    chosen = (ids == expert) & (keep == 1)
    picked = jnp.any(chosen, axis=1)
    position = jnp.cumsum(picked.astype(jnp.int32)) - 1
    return chosen, picked, position


def body(states, expert_ids, gate_values, keep_mask, w_gate, w_up, w_down):
    tokens = states[0]
    ids, gates, keep = expert_ids[0], gate_values[0], keep_mask[0]
    matrices = (w_gate[0], w_up[0], w_down[0])
    mine = lax.axis_index("yh")
    other = 1 - mine

    def compact(expert, tokens):
        _, picked, position = slots(ids, keep, expert)
        table = (position[None] == jnp.arange(CAP, dtype=jnp.int32)[:, None]) & picked[None]
        return jnp.dot(table.astype(BF16), tokens, preferred_element_type=F32).astype(BF16)

    others, tokens = together(compact(other, tokens), tokens)
    partner = to_partner(others)
    own = compact(mine, tokens)

    a1, b = split(own, 2)
    a1_y, b_behind, b_ahead = over_y(a1), right(b), left(b)
    a1_near = join(a1, a1_y)
    a1_far, b_opposite = over_z(a1_near), right(b_behind)
    a1_near_left, a1_near_right = right(a1_near), left(a1_near)
    b_ring = join(b, b_behind, b_ahead, b_opposite)
    b_y = over_y(b_ring)

    a2, g = split(partner, 2)
    a2_z, g_behind, g_ahead = over_z(a2), left(g), right(g)
    g_behind, g_ahead, b_ring_late, a1_far_late = together(g_behind, g_ahead, b_ring, a1_far)
    g_opposite = left(g_behind)
    b_z = over_z(b_ring_late)
    a1_far_left, a1_far_right = right(a1_far_late), left(a1_far_late)
    a2_near = join(a2, a2_z)
    a2_far = over_y(a2_near)
    g_opposite, a2_near_late = together(g_opposite, a2_near)
    a2_near_left, a2_near_right = right(a2_near_late), left(a2_near_late)
    g_ring = join(g, g_behind, g_ahead, g_opposite)
    b_y, g_ring = together(b_y, g_ring)
    g_y, g_z = over_y(g_ring), over_z(g_ring)

    a1_near, a1_far, b_ring, b_y, p_near_left, p_near_right = experts(
        [a1_near, a1_far, b_ring, b_y, a1_near_left, a1_near_right], *matrices
    )
    a1_near_left, a1_far_right, b_z, a2_far, a1_near = together(
        a1_near_left, a1_far_right, b_z, a2_far, a1_near
    )
    a1_near_opposite, a1_far_opposite = right(a1_near_left), left(a1_far_right)
    a2_far_left, a2_far_right = right(a2_far), left(a2_far)
    b_yz = over_y(b_z)
    a1_near_left, a1_near_right = p_near_left, p_near_right
    g_ring, a2_near, a2_far, a1_far_left, p_far_right, b_z = experts(
        [g_ring, a2_near, a2_far, a1_far_left, a1_far_right, b_z], *matrices
    )
    a1_far_right = p_far_right
    a2_near_left, a2_far_right, g_y, g_z, a1_near_opposite, a1_far_opposite, g_ring = together(
        a2_near_left, a2_far_right, g_y, g_z, a1_near_opposite, a1_far_opposite, g_ring
    )
    a2_near_opposite, a2_far_opposite = right(a2_near_left), left(a2_far_right)
    g_zy = over_z(g_y)
    a2_near_left, a2_near_right, a1_near_opposite, a1_far_opposite, g_y, g_z = experts(
        [a2_near_left, a2_near_right, a1_near_opposite, a1_far_opposite, g_y, g_z], *matrices
    )
    last = together(a2_far_left, a2_far_right, a2_near_opposite, a2_far_opposite, b_yz, g_zy, g_y)
    g_y = last[-1]

    a1_near_opposite, a1_far_opposite, a1_near_right, a1_far_left, b_y, g_own = together(
        left(a1_near_opposite), right(a1_far_opposite), right(a1_near_right), left(a1_far_left),
        over_y(b_y), over_z(g_ring),
    )
    a2_far_left, a2_far_right, a2_near_opposite, a2_far_opposite, b_yz, g_zy = experts(
        list(last[:-1]), *matrices
    )
    (
        a1_near_opposite, a1_far_opposite, a1_near_right, a1_far_left, b_y, g_own, g_y,
        a2_near_opposite, a2_far_opposite, b_yz,
    ) = together(
        a1_near_opposite, a1_far_opposite, a1_near_right, a1_far_left, b_y, g_own, g_y,
        a2_near_opposite, a2_far_opposite, b_yz,
    )
    g_y_back, b_yz_back = over_z(g_y), over_y(b_yz)
    a2_near_opposite, a2_far_opposite = left(a2_near_opposite), right(a2_far_opposite)
    a1_near_left = left(add(a1_near_left, a1_near_opposite))
    a1_far_right = right(add(a1_far_right, a1_far_opposite))
    b_ring = add(b_ring, b_y)
    g_y_back, b_yz_back, a2_near_opposite, a2_far_opposite, b_ring, ids, gates, keep = together(
        g_y_back, b_yz_back, a2_near_opposite, a2_far_opposite, b_ring, ids, gates, keep
    )

    b_own, g_zy_back = over_z(b_ring), over_y(add(g_zy, g_y_back))
    a2_near_right, a2_far_left = right(a2_near_right), left(a2_far_left)
    a2_near_left = left(add(a2_near_left, a2_near_opposite))
    a2_far_right = right(add(a2_far_right, a2_far_opposite))
    ids, gates, keep = (to_next_section(v) for v in (ids, gates, keep))
    a1_near = add(a1_near, a1_near_left, a1_near_right)
    (
        a1_near, a1_far, b_z, b_yz_back, b_own, g_z, g_own, g_zy_back,
        a2_near_left, a2_near_right, a2_far_left, a2_far_right,
    ) = together(
        a1_near, add(a1_far, a1_far_left, a1_far_right), b_z, b_yz_back, b_own, g_z, g_own, g_zy_back,
        a2_near_left, a2_near_right, a2_far_left, a2_far_right,
    )

    def part(terms, i, count):
        return [t[i * t.shape[0] // count : (i + 1) * t.shape[0] // count] for t in terms]

    b_terms, g_terms = (b_z, b_yz_back, b_own), (g_z, g_own, g_zy_back)
    a2_near_terms = (a2_near, a2_near_left, a2_near_right)
    got = together(
        left(join(add(*part(b_terms, 3, 4)), add(*part(g_terms, 2, 4)))),
        right(join(add(*part(g_terms, 3, 4)), add(*part(b_terms, 2, 4)))),
        over_z(a1_near),
        over_y(add(a2_far, a2_far_left, a2_far_right)),
    )
    (b_behind_back, g_back), (g_behind_back, b_back) = split(got[0], 2), split(got[1], 2)
    a1_terms, a2_terms = (a1_far, got[2]), (*a2_near_terms, got[3])
    ends = together(
        left(add(*part(b_terms, 1, 4), b_behind_back)),
        right(add(*part(g_terms, 1, 4), g_behind_back)),
        over_y(add(*part(a1_terms, 1, 2))),
        over_z(add(*part(a2_terms, 0, 2))),
    )

    own_done = to_owner(
        join(add(*part(a1_terms, 0, 2), ends[2]), add(*part(b_terms, 0, 4), b_back, ends[0]))
    )
    other_done = to_owner_across(
        join(add(*part(a2_terms, 1, 2), ends[3]), add(*part(g_terms, 0, 4), g_back, ends[1]))
    )

    def contribution(expert, done):
        chosen, picked, position = slots(ids, keep, expert)
        weight = jnp.sum(jnp.where(chosen, gates, 0.0), axis=1)
        table = (position[:, None] == jnp.arange(CAP, dtype=jnp.int32)[None]) & picked[:, None]
        rows = jnp.dot(table.astype(BF16), done, preferred_element_type=F32)
        return weight[:, None] * rows

    mixed = contribution(mine, own_done) + contribution(other, other_done)
    return mixed.astype(BF16)[None]


def solution(mesh):
    shape = (2, 2, 2, 2, 4, 2)
    fine = Mesh(mesh.devices.reshape(shape), ("zh", "core", "yh", "yl", "x", "zl"))
    section, ep = ("zh", "core"), ("yh", "yl", "x", "zl")
    rows = P(section, ep, None)
    columns = P(section, None, ep)
    return jax.shard_map(
        body,
        mesh=fine,
        in_specs=(rows, rows, rows, rows, columns, columns, rows),
        out_specs=rows,
        check_vma=False,
    )
```

```python
import jax
import jax.numpy as jnp
from jax import lax
from jax.experimental import pallas as pl
from jax.experimental.pallas import tpu as pltpu
from jax.sharding import Mesh, PartitionSpec as P

CAP = 48
PIECE = 24
F32 = jnp.float32
BF16 = jnp.bfloat16


def shift(value, axis, by):
    n = lax.axis_size(axis)
    return lax.ppermute(value, axis, [(i, (i + by) % n) for i in range(n)])


def right(value):
    return shift(value, "x", 1)


def left(value):
    return shift(value, "x", -1)


def over_y(value):
    return shift(value, "yl", 1)


def over_z(value):
    return shift(value, "zl", 1)


def to_partner(value):
    return lax.ppermute(value, ("yh", "yl"), [(y, 3 - y) for y in range(4)])


def to_next_section(value):
    return lax.ppermute(value, ("zh", "core"), [(s, (s + 1) % 4) for s in range(4)])


def to_owner(value):
    pairs = [(s * 2 + z, (s + 1) % 4 * 2 + 1 - z) for s in range(4) for z in range(2)]
    return lax.ppermute(value, ("zh", "core", "zl"), pairs)


def to_owner_across(value):
    pairs = [
        ((s * 4 + y) * 2 + z, ((s + 1) % 4 * 4 + 3 - y) * 2 + 1 - z)
        for s in range(4)
        for y in range(4)
        for z in range(2)
    ]
    return lax.ppermute(value, ("zh", "core", "yh", "yl", "zl"), pairs)


def together(*values):
    return lax.optimization_barrier(values)


def join(*pieces):
    return jnp.concatenate(pieces)


def add(*terms):
    total = terms[0].astype(F32)
    for term in terms[1:]:
        total = total + term.astype(F32)
    return total.astype(BF16)


def split(rows, count):
    size = rows.shape[0] // count
    return [rows[i * size : (i + 1) * size] for i in range(count)]


def take(arrays, part, parts):
    return [(array, part, array.shape[0] // parts) for array in arrays]


def sums(*wanted):
    width = wanted[0][0][0][0].shape[1]
    tile = width // 2
    blocks = [term for segments in wanted for terms in segments for term in terms]
    heights = [sum(terms[0][2] for terms in segments) for segments in wanted]

    def kernel(*refs):
        ins, outs = iter(refs[: len(blocks)]), refs[len(blocks) :]
        for segments, out in zip(wanted, outs):
            start = 0
            for terms in segments:
                total = next(ins)[...].astype(F32)
                for _ in terms[1:]:
                    total = total + next(ins)[...].astype(F32)
                out[start : start + terms[0][2]] = total.astype(BF16)
                start += terms[0][2]

    return pl.pallas_call(
        kernel,
        grid=(width // tile,),
        in_specs=[pl.BlockSpec((n, tile), lambda i, part=part: (part, i)) for _, part, n in blocks],
        out_specs=[pl.BlockSpec((n, tile), lambda i: (0, i)) for n in heights],
        out_shape=[jax.ShapeDtypeStruct((n, width), BF16) for n in heights],
        compiler_params=pltpu.CompilerParams(dimension_semantics=("arbitrary",)),
        name="sums",
    )(*[array for array, _, _ in blocks])


TILE = 1536


def experts_kernel(*refs):
    count = (len(refs) - 6) // 2
    rows, (w_gate, w_up, w_down), rest = refs[:count], refs[count : count + 3], refs[count + 3 :]
    outs, (gate, up, hidden) = rest[:count], rest[count:]
    step = pl.program_id(0)
    half = pl.num_programs(0) // 2

    @pl.when(step < half)
    def _():
        block = jnp.concatenate([r[...] for r in rows])
        gate_part = jnp.dot(block, w_gate[...], preferred_element_type=F32)
        up_part = jnp.dot(block, w_up[...], preferred_element_type=F32)

        @pl.when(step == 0)
        def _():
            gate[...] = gate_part
            up[...] = up_part

        @pl.when(step > 0)
        def _():
            gate[...] += gate_part
            up[...] += up_part

    @pl.when(step >= half)
    def _():
        @pl.when(step == half)
        def _():
            v = gate[...]
            hidden[...] = (v / (1.0 + jnp.exp(-v)) * up[...]).astype(BF16)

        out = jnp.dot(hidden[...], w_down[...], preferred_element_type=F32).astype(BF16)
        start = 0
        for o in outs:
            o[...] = out[start : start + o.shape[0]]
            start += o.shape[0]


def experts(pieces, gate_matrix, up_matrix, down_matrix):
    sizes, width = [p.shape[0] for p in pieces], pieces[0].shape[1]
    units = gate_matrix.shape[1]
    half = width // TILE
    first = lambda i: jnp.minimum(i, half - 1)
    second = lambda i: jnp.maximum(i - half, 0)
    rows_in = [pl.BlockSpec((n, TILE), lambda i: (0, first(i))) for n in sizes]
    rows_out = [pl.BlockSpec((n, TILE), lambda i: (0, second(i))) for n in sizes]
    into = pl.BlockSpec((TILE, units), lambda i: (first(i), 0))
    out_of = pl.BlockSpec((units, TILE), lambda i: (0, second(i)))
    total = sum(sizes)
    return pl.pallas_call(
        experts_kernel,
        grid=(2 * half,),
        in_specs=rows_in + [into, into, out_of],
        out_specs=rows_out,
        out_shape=[jax.ShapeDtypeStruct((n, width), BF16) for n in sizes],
        scratch_shapes=[
            pltpu.VMEM((total, units), F32),
            pltpu.VMEM((total, units), F32),
            pltpu.VMEM((total, units), BF16),
        ],
        compiler_params=pltpu.CompilerParams(
            dimension_semantics=("arbitrary",), vmem_limit_bytes=24 << 20
        ),
        cost_estimate=pl.CostEstimate(
            flops=6 * total * width * units,
            transcendentals=total * units,
            bytes_accessed=6 * width * units + 4 * total * width,
        ),
        name="experts",
    )(*pieces, *(pltpu.with_memory_space_constraint(m, pltpu.HBM) for m in (gate_matrix, up_matrix, down_matrix)))


def body(states, expert_ids, gate_values, keep_mask, w_gate, w_up, w_down):
    tokens = states[0]
    ids, gates, keep = expert_ids[0], gate_values[0], keep_mask[0]
    matrices = (w_gate[0], w_up[0], w_down[0])
    mine = lax.axis_index("yh")
    other = 1 - mine

    def slots(expert):
        chosen = (ids == expert) & (keep == 1)
        picked = jnp.any(chosen, axis=1)
        position = jnp.where(picked, jnp.cumsum(picked.astype(jnp.int32)) - 1, -1)
        return position, jnp.sum(jnp.where(chosen, gates, 0.0), axis=1)

    def compact(position, tokens):
        table = position[None] == jnp.arange(CAP, dtype=jnp.int32)[:, None]
        return jnp.dot(table.astype(BF16), tokens, preferred_element_type=F32).astype(BF16)

    (mine_at, mine_weight), (other_at, other_weight) = slots(mine), slots(other)
    info = jnp.stack([mine_at.astype(F32), other_at.astype(F32), mine_weight, other_weight])

    others, tokens = together(compact(other_at, tokens), tokens)
    partner = to_partner(others)
    own = compact(mine_at, tokens)

    a1, b = split(own, 2)
    a1_y, b_behind, b_ahead = over_y(a1), right(b), left(b)
    a1_near = join(a1, a1_y)
    a1_far, b_opposite = over_z(a1_near), right(b_behind)
    b_ring = join(b, b_behind, b_ahead, b_opposite)

    a2, g = split(partner, 2)
    a2_z, g_behind, g_ahead = over_z(a2), left(g), right(g)
    b_y = over_y(b_ring)
    g_behind, g_ahead, b_ring_z = together(g_behind, g_ahead, b_ring)
    g_opposite = left(g_behind)
    a2_near = join(a2, a2_z)
    near = join(a1_near, a2_near)
    a2_far, b_z = over_y(a2_near), over_z(b_ring_z)
    near_late, g_opposite_done = together(near, g_opposite)
    near_left, near_right = right(near), left(near_late)
    g_ring = join(g, g_behind, g_ahead, g_opposite_done)

    b_y, g_ring_out = together(b_y, g_ring)
    g_y, g_z = over_y(g_ring_out), over_z(g_ring_out)
    far = join(a1_far, a2_far)
    near, b_ring, g_ring, b_y = experts([near, b_ring, g_ring, b_y], *matrices)
    far_left, far_right = right(far), left(far)

    near_left, near_right, far, b_z, near, b_ring, g_ring, b_y = together(
        near_left, near_right, far, b_z, near, b_ring, g_ring, b_y
    )
    near_opposite, b_yz = right(near_left), over_y(b_z)
    near_left, near_right, far, b_z = experts([near_left, near_right, far, b_z], *matrices)

    far_left, far_right, g_y, g_z, near_left, near_right, far, b_z = together(
        far_left, far_right, g_y, g_z, near_left, near_right, far, b_z
    )
    far_opposite, g_zy = left(far_right), over_z(g_y)
    far_left, far_right, g_y, g_z = experts([far_left, far_right, g_y, g_z], *matrices)

    near_opposite, far_opposite, b_yz, g_zy, far_left, far_right, g_y, g_z = together(
        near_opposite, far_opposite, b_yz, g_zy, far_left, far_right, g_y, g_z
    )
    near_back, far_back, b_back, g_own = (
        right(near_right), left(far_left), over_y(b_y), over_z(g_ring)
    )
    near_opposite, far_opposite, b_yz, g_zy = experts(
        [near_opposite, far_opposite, b_yz, g_zy], *matrices
    )
    near_opposite, far_opposite, b_yz, g_y, near_back, far_back, b_back, g_own = together(
        near_opposite, far_opposite, b_yz, g_y, near_back, far_back, b_back, g_own
    )
    got = left(near_opposite), right(far_opposite), over_y(b_yz), over_z(g_y)
    near_left, far_right = add(near_left, got[0]), add(far_right, got[1])
    b_ring, g_zy = add(b_ring, b_back), add(g_zy, got[3])
    info, b_yz_back, near_left, far_right, b_ring, g_zy = together(
        info, got[2], near_left, far_right, b_ring, g_zy
    )
    *got, info = together(
        left(near_left), right(far_right), over_z(b_ring), over_y(g_zy), to_next_section(info)
    )

    near, far = (near, near_back, got[0]), (far, far_back, got[1])
    b_terms, g_terms = (b_z, b_yz_back, got[2]), (g_z, g_own, got[3])
    got = sums(
        [take(b_terms, 3, 4), take(g_terms, 2, 4)],
        [take(g_terms, 3, 4), take(b_terms, 2, 4)],
        [take(near, 0, 2)],
        [take(far, 1, 2)],
    )
    got = together(left(got[0]), right(got[1]), over_z(got[2]), over_y(got[3]))
    a1_terms = take(far, 0, 4), take(far, 1, 4)
    a2_terms = take(near, 2, 4), take(near, 3, 4)
    ends = sums(
        [take(b_terms, 1, 4) + take(got[:1], 0, 2)],
        [take(g_terms, 1, 4) + take(got[1:2], 0, 2)],
        [a1_terms[1] + take(got[2:3], 1, 2)],
        [a2_terms[0] + take(got[3:], 0, 2)],
    )
    ends = together(left(ends[0]), right(ends[1]), over_y(ends[2]), over_z(ends[3]))
    own, partner = sums(
        [
            a1_terms[0] + take(got[2:3], 0, 2) + take(ends[2:3], 0, 1),
            take(b_terms, 0, 4) + take(got[1:2], 1, 2) + take(ends[:1], 0, 1),
        ],
        [
            a2_terms[1] + take(got[3:], 1, 2) + take(ends[3:], 0, 1),
            take(g_terms, 0, 4) + take(got[:1], 1, 2) + take(ends[1:2], 0, 1),
        ],
    )

    own_done, other_done = to_owner(own), to_owner_across(partner)

    def contribution(position, weight, done):
        table = position[:, None] == jnp.arange(CAP, dtype=F32)[None]
        rows = jnp.dot(table.astype(BF16), done, preferred_element_type=F32)
        return weight[:, None] * rows

    mixed = contribution(info[0], info[2], own_done) + contribution(info[1], info[3], other_done)
    return mixed.astype(BF16)[None]


def solution(mesh):
    shape = (2, 2, 2, 2, 4, 2)
    fine = Mesh(mesh.devices.reshape(shape), ("zh", "core", "yh", "yl", "x", "zl"))
    section, ep = ("zh", "core"), ("yh", "yl", "x", "zl")
    rows = P(section, ep, None)
    columns = P(section, None, ep)
    return jax.shard_map(
        body,
        mesh=fine,
        in_specs=(rows, rows, rows, rows, columns, columns, rows),
        out_specs=rows,
        check_vma=False,
    )
```

```python
import jax
import jax.numpy as jnp
from jax import lax
from jax.experimental import pallas as pl
from jax.experimental.pallas import tpu as pltpu
from jax.sharding import Mesh, PartitionSpec as P

CAP = 48
PIECE = 24
F32 = jnp.float32
BF16 = jnp.bfloat16


def shift(value, axis, by):
    n = lax.axis_size(axis)
    return lax.ppermute(value, axis, [(i, (i + by) % n) for i in range(n)])


def right(value):
    return shift(value, "x", 1)


def left(value):
    return shift(value, "x", -1)


def over_y(value):
    return shift(value, "yl", 1)


def over_z(value):
    return shift(value, "zl", 1)


def to_partner(value):
    return lax.ppermute(value, ("yh", "yl"), [(y, 3 - y) for y in range(4)])


def to_next_section(value):
    return lax.ppermute(value, ("zh", "core"), [(s, (s + 1) % 4) for s in range(4)])


def to_owner(value):
    pairs = [(s * 2 + z, (s + 1) % 4 * 2 + 1 - z) for s in range(4) for z in range(2)]
    return lax.ppermute(value, ("zh", "core", "zl"), pairs)


def to_owner_across(value):
    pairs = [
        ((s * 4 + y) * 2 + z, ((s + 1) % 4 * 4 + 3 - y) * 2 + 1 - z)
        for s in range(4)
        for y in range(4)
        for z in range(2)
    ]
    return lax.ppermute(value, ("zh", "core", "yh", "yl", "zl"), pairs)


def together(*values):
    return lax.optimization_barrier(values)


def join(*pieces):
    return jnp.concatenate(pieces)


def add(*terms):
    total = terms[0].astype(F32)
    for term in terms[1:]:
        total = total + term.astype(F32)
    return total.astype(BF16)


def split(rows, count):
    size = rows.shape[0] // count
    return [rows[i * size : (i + 1) * size] for i in range(count)]


def take(arrays, part, parts):
    return [(array, part, array.shape[0] // parts) for array in arrays]


def sums(*wanted):
    pick = lambda array, part, rows: array[part * rows : (part + 1) * rows]
    out = []
    for segments in wanted:
        out.append(join(*(add(*(pick(*term) for term in terms)) for terms in segments)))
    return out


TILE = 1536


def experts_kernel(*refs):
    count = (len(refs) - 6) // 2
    rows, (w_gate, w_up, w_down), rest = refs[:count], refs[count : count + 3], refs[count + 3 :]
    outs, (gate, up, hidden) = rest[:count], rest[count:]
    step = pl.program_id(0)
    half = pl.num_programs(0) // 2

    @pl.when(step < half)
    def _():
        block = jnp.concatenate([r[...] for r in rows])
        gate_part = jnp.dot(block, w_gate[...], preferred_element_type=F32)
        up_part = jnp.dot(block, w_up[...], preferred_element_type=F32)

        @pl.when(step == 0)
        def _():
            gate[...] = gate_part
            up[...] = up_part

        @pl.when(step > 0)
        def _():
            gate[...] += gate_part
            up[...] += up_part

    @pl.when(step >= half)
    def _():
        @pl.when(step == half)
        def _():
            v = gate[...]
            hidden[...] = (v / (1.0 + jnp.exp(-v)) * up[...]).astype(BF16)

        out = jnp.dot(hidden[...], w_down[...], preferred_element_type=F32).astype(BF16)
        start = 0
        for o in outs:
            o[...] = out[start : start + o.shape[0]]
            start += o.shape[0]


def experts(pieces, gate_matrix, up_matrix, down_matrix):
    sizes, width = [p.shape[0] for p in pieces], pieces[0].shape[1]
    units = gate_matrix.shape[1]
    half = width // TILE
    first = lambda i: jnp.minimum(i, half - 1)
    second = lambda i: jnp.maximum(i - half, 0)
    rows_in = [pl.BlockSpec((n, TILE), lambda i: (0, first(i))) for n in sizes]
    rows_out = [pl.BlockSpec((n, TILE), lambda i: (0, second(i))) for n in sizes]
    into = pl.BlockSpec((TILE, units), lambda i: (first(i), 0))
    out_of = pl.BlockSpec((units, TILE), lambda i: (0, second(i)))
    total = sum(sizes)
    return pl.pallas_call(
        experts_kernel,
        grid=(2 * half,),
        in_specs=rows_in + [into, into, out_of],
        out_specs=rows_out,
        out_shape=[jax.ShapeDtypeStruct((n, width), BF16) for n in sizes],
        scratch_shapes=[
            pltpu.VMEM((total, units), F32),
            pltpu.VMEM((total, units), F32),
            pltpu.VMEM((total, units), BF16),
        ],
        compiler_params=pltpu.CompilerParams(
            dimension_semantics=("arbitrary",), vmem_limit_bytes=18 << 20
        ),
        cost_estimate=pl.CostEstimate(
            flops=6 * total * width * units,
            transcendentals=total * units,
            bytes_accessed=6 * width * units + 4 * total * width,
        ),
        name="experts",
    )(*pieces, gate_matrix, up_matrix, down_matrix)


def body(states, expert_ids, gate_values, keep_mask, w_gate, w_up, w_down):
    tokens = states[0]
    ids, gates, keep = expert_ids[0], gate_values[0], keep_mask[0]
    matrices = (w_gate[0], w_up[0], w_down[0])
    mine = lax.axis_index("yh")
    other = 1 - mine

    def slots(expert):
        chosen = (ids == expert) & (keep == 1)
        picked = jnp.any(chosen, axis=1)
        position = jnp.where(picked, jnp.cumsum(picked.astype(jnp.int32)) - 1, -1)
        return position, jnp.sum(jnp.where(chosen, gates, 0.0), axis=1)

    def compact(position, tokens):
        table = position[None] == jnp.arange(CAP, dtype=jnp.int32)[:, None]
        return jnp.dot(table.astype(BF16), tokens, preferred_element_type=F32).astype(BF16)

    (mine_at, mine_weight), (other_at, other_weight) = slots(mine), slots(other)
    info = jnp.stack([mine_at.astype(F32), other_at.astype(F32), mine_weight, other_weight])

    others, tokens = together(compact(other_at, tokens), tokens)
    partner = to_partner(others)
    own = compact(mine_at, tokens)

    a1, b = split(own, 2)
    a1_y, b_behind, b_ahead = over_y(a1), right(b), left(b)
    a1_near = join(a1, a1_y)
    b_opposite = right(b_behind)
    b_ring = join(b, b_behind, b_ahead, b_opposite)
    b_y = over_y(b_ring)

    a2, g = split(partner, 2)
    a2_z, g_behind, g_ahead = over_z(a2), left(g), right(g)
    g_behind, g_ahead, b_ring_late, a1_near_late = together(g_behind, g_ahead, b_ring, a1_near)
    g_opposite = left(g_behind)
    a1_far = over_z(a1_near_late)
    a2_near = join(a2, a2_z)
    near = join(a1_near, a2_near)
    a1_far, b_ring_late = together(a1_far, b_ring_late)
    a2_far, b_z = over_y(a2_near), over_z(b_ring_late)
    near_late, g_opposite = together(near, g_opposite)
    near_left, near_right = right(near), left(near_late)
    g_ring = join(g, g_behind, g_ahead, g_opposite)

    b_y, g_ring_out = together(b_y, g_ring)
    g_y, g_z = over_y(g_ring_out), over_z(g_ring_out)
    far = join(a1_far, a2_far)
    near, b_ring, g_ring, b_y = experts([near, b_ring, g_ring, b_y], *matrices)
    far_left, far_right = right(far), left(far)

    near_left, near_right, far, b_z, near, b_ring, g_ring, b_y = together(
        near_left, near_right, far, b_z, near, b_ring, g_ring, b_y
    )
    near_opposite, b_yz = left(near_right), over_y(b_z)
    near_left, near_right, far, b_z = experts([near_left, near_right, far, b_z], *matrices)

    far_left, far_right, g_y, g_z, near_left, near_right, far, b_z = together(
        far_left, far_right, g_y, g_z, near_left, near_right, far, b_z
    )
    far_opposite, g_zy = right(far_left), over_z(g_y)
    far_left, far_right, g_y, g_z = experts([far_left, far_right, g_y, g_z], *matrices)

    near_opposite, far_opposite, b_yz, g_zy, far_left, far_right, g_y, g_z = together(
        near_opposite, far_opposite, b_yz, g_zy, far_left, far_right, g_y, g_z
    )
    near_back, far_back, b_back, g_own = (
        left(near_left), right(far_right), over_y(b_y), over_z(g_ring)
    )
    near_opposite, far_opposite, b_yz, g_zy = experts(
        [near_opposite, far_opposite, b_yz, g_zy], *matrices
    )
    near_opposite, far_opposite, b_yz, g_y, near_back, far_back, b_back, g_own = together(
        near_opposite, far_opposite, b_yz, g_y, near_back, far_back, b_back, g_own
    )
    got = right(near_opposite), left(far_opposite), over_y(b_yz), over_z(g_y)
    near_right, far_left = add(near_right, got[0]), add(far_left, got[1])
    b_ring, g_zy = add(b_ring, b_back), add(g_zy, got[3])
    info, b_yz_back, near_right, far_left, b_ring, g_zy = together(
        info, got[2], near_right, far_left, b_ring, g_zy
    )
    *got, info = together(
        right(near_right), left(far_left), over_z(b_ring), over_y(g_zy), to_next_section(info)
    )

    near, far = (near, near_back, got[0]), (far, far_back, got[1])
    b_terms, g_terms = (b_z, b_yz_back, got[2]), (g_z, g_own, got[3])
    got = sums(
        [take(b_terms, 3, 4), take(g_terms, 2, 4)],
        [take(g_terms, 3, 4), take(b_terms, 2, 4)],
        [take(near, 0, 2)],
        [take(far, 1, 2)],
    )
    got = together(left(got[0]), right(got[1]), over_z(got[2]), over_y(got[3]))
    a1_terms = take(far, 0, 4), take(far, 1, 4)
    a2_terms = take(near, 2, 4), take(near, 3, 4)
    ends = sums(
        [take(b_terms, 1, 4) + take(got[:1], 0, 2)],
        [take(g_terms, 1, 4) + take(got[1:2], 0, 2)],
        [a1_terms[1] + take(got[2:3], 1, 2)],
        [a2_terms[0] + take(got[3:], 0, 2)],
    )
    ends = together(left(ends[0]), right(ends[1]), over_y(ends[2]), over_z(ends[3]))
    own, partner = sums(
        [
            a1_terms[0] + take(got[2:3], 0, 2) + take(ends[2:3], 0, 1),
            take(b_terms, 0, 4) + take(got[1:2], 1, 2) + take(ends[:1], 0, 1),
        ],
        [
            a2_terms[1] + take(got[3:], 1, 2) + take(ends[3:], 0, 1),
            take(g_terms, 0, 4) + take(got[:1], 1, 2) + take(ends[1:2], 0, 1),
        ],
    )

    own_done, other_done = to_owner(own), to_owner_across(partner)

    def contribution(position, weight, done):
        table = position[:, None] == jnp.arange(CAP, dtype=F32)[None]
        rows = jnp.dot(table.astype(BF16), done, preferred_element_type=F32)
        return weight[:, None] * rows

    mixed = contribution(info[0], info[2], own_done) + contribution(info[1], info[3], other_done)
    return mixed.astype(BF16)[None]


def solution(mesh):
    shape = (2, 2, 2, 2, 4, 2)
    fine = Mesh(mesh.devices.reshape(shape), ("zh", "core", "yh", "yl", "x", "zl"))
    section, ep = ("zh", "core"), ("yh", "yl", "x", "zl")
    rows = P(section, ep, None)
    columns = P(section, None, ep)
    return jax.shard_map(
        body,
        mesh=fine,
        in_specs=(rows, rows, rows, rows, columns, columns, rows),
        out_specs=rows,
        check_vma=False,
    )
```

```python
import jax
import jax.numpy as jnp
from jax import lax
from jax.experimental import pallas as pl
from jax.experimental.pallas import tpu as pltpu
from jax.sharding import Mesh, PartitionSpec as P

CAP = 48
PIECE = 24
F32 = jnp.float32
BF16 = jnp.bfloat16


def shift(value, axis, by):
    n = lax.axis_size(axis)
    return lax.ppermute(value, axis, [(i, (i + by) % n) for i in range(n)])


def right(value):
    return shift(value, "x", 1)


def left(value):
    return shift(value, "x", -1)


def over_y(value):
    return shift(value, "yl", 1)


def over_z(value):
    return shift(value, "zl", 1)


def to_partner(value):
    return lax.ppermute(value, ("yh", "yl"), [(y, 3 - y) for y in range(4)])


def to_next_section(value):
    return lax.ppermute(value, ("zh", "core"), [(s, (s + 1) % 4) for s in range(4)])


def to_owner(value):
    pairs = [(s * 2 + z, (s + 1) % 4 * 2 + 1 - z) for s in range(4) for z in range(2)]
    return lax.ppermute(value, ("zh", "core", "zl"), pairs)


def to_owner_across(value):
    pairs = [
        ((s * 4 + y) * 2 + z, ((s + 1) % 4 * 4 + 3 - y) * 2 + 1 - z)
        for s in range(4)
        for y in range(4)
        for z in range(2)
    ]
    return lax.ppermute(value, ("zh", "core", "yh", "yl", "zl"), pairs)


def together(*values):
    return lax.optimization_barrier(values)


def join(*pieces):
    return jnp.concatenate(pieces)


def add(*terms):
    total = terms[0].astype(F32)
    for term in terms[1:]:
        total = total + term.astype(F32)
    return total.astype(BF16)


def split(rows, count):
    size = rows.shape[0] // count
    return [rows[i * size : (i + 1) * size] for i in range(count)]


def take(arrays, part, parts):
    return [(array, part, array.shape[0] // parts) for array in arrays]


def sums(*wanted):
    pick = lambda array, part, rows: array[part * rows : (part + 1) * rows]
    out = []
    for segments in wanted:
        out.append(join(*(add(*(pick(*term) for term in terms)) for terms in segments)))
    return out


TILE = 1536


def experts_kernel(*refs):
    count = (len(refs) - 6) // 2
    rows, (w_gate, w_up, w_down), rest = refs[:count], refs[count : count + 3], refs[count + 3 :]
    outs, (gate, up, hidden) = rest[:count], rest[count:]
    step = pl.program_id(0)
    half = pl.num_programs(0) // 2

    @pl.when(step < half)
    def _():
        block = jnp.concatenate([r[...] for r in rows])
        gate_part = jnp.dot(block, w_gate[...], preferred_element_type=F32)
        up_part = jnp.dot(block, w_up[...], preferred_element_type=F32)

        @pl.when(step == 0)
        def _():
            gate[...] = gate_part
            up[...] = up_part

        @pl.when(step > 0)
        def _():
            gate[...] += gate_part
            up[...] += up_part

    @pl.when(step >= half)
    def _():
        @pl.when(step == half)
        def _():
            v = gate[...]
            hidden[...] = (v / (1.0 + jnp.exp(-v)) * up[...]).astype(BF16)

        out = jnp.dot(hidden[...], w_down[...], preferred_element_type=F32).astype(BF16)
        start = 0
        for o in outs:
            o[...] = out[start : start + o.shape[0]]
            start += o.shape[0]


def experts(pieces, gate_matrix, up_matrix, down_matrix):
    sizes, width = [p.shape[0] for p in pieces], pieces[0].shape[1]
    units = gate_matrix.shape[1]
    half = width // TILE
    first = lambda i: jnp.minimum(i, half - 1)
    second = lambda i: jnp.maximum(i - half, 0)
    rows_in = [pl.BlockSpec((n, TILE), lambda i: (0, first(i))) for n in sizes]
    rows_out = [pl.BlockSpec((n, TILE), lambda i: (0, second(i))) for n in sizes]
    into = pl.BlockSpec((TILE, units), lambda i: (first(i), 0))
    out_of = pl.BlockSpec((units, TILE), lambda i: (0, second(i)))
    total = sum(sizes)
    return pl.pallas_call(
        experts_kernel,
        grid=(2 * half,),
        in_specs=rows_in + [into, into, out_of],
        out_specs=rows_out,
        out_shape=[jax.ShapeDtypeStruct((n, width), BF16) for n in sizes],
        scratch_shapes=[
            pltpu.VMEM((total, units), F32),
            pltpu.VMEM((total, units), F32),
            pltpu.VMEM((total, units), BF16),
        ],
        compiler_params=pltpu.CompilerParams(
            dimension_semantics=("arbitrary",), vmem_limit_bytes=18 << 20
        ),
        cost_estimate=pl.CostEstimate(
            flops=6 * total * width * units,
            transcendentals=total * units,
            bytes_accessed=6 * width * units + 4 * total * width,
        ),
        name="experts",
    )(*pieces, gate_matrix, up_matrix, down_matrix)


def body(states, expert_ids, gate_values, keep_mask, w_gate, w_up, w_down):
    tokens = states[0]
    ids, gates, keep = expert_ids[0], gate_values[0], keep_mask[0]
    matrices = (w_gate[0], w_up[0], w_down[0])
    mine = lax.axis_index("yh")
    other = 1 - mine

    def slots(expert):
        chosen = (ids == expert) & (keep == 1)
        picked = jnp.any(chosen, axis=1)
        position = jnp.where(picked, jnp.cumsum(picked.astype(jnp.int32)) - 1, -1)
        return position, jnp.sum(jnp.where(chosen, gates, 0.0), axis=1)

    def compact(position, tokens):
        table = position[None] == jnp.arange(CAP, dtype=jnp.int32)[:, None]
        return jnp.dot(table.astype(BF16), tokens, preferred_element_type=F32).astype(BF16)

    (mine_at, mine_weight), (other_at, other_weight) = slots(mine), slots(other)
    info = jnp.stack([mine_at.astype(F32), other_at.astype(F32), mine_weight, other_weight])

    others, tokens = together(compact(other_at, tokens), tokens)
    partner = to_partner(others)
    own = compact(mine_at, tokens)

    a1, b = split(own, 2)
    a1_y, b_behind, b_ahead = over_y(a1), right(b), left(b)
    a1_near = join(a1, a1_y)
    a1_far, b_opposite = over_z(a1_near), right(b_behind)
    partner, b_ahead, b_opposite = together(partner, b_ahead, b_opposite)
    b_ring = join(b, b_behind, b_ahead, b_opposite)
    b_z = over_z(b_ring)

    a2, g = split(partner, 2)
    a2_y, g_behind, g_ahead = over_y(a2), left(g), right(g)
    g_behind, g_ahead, b_ring_late = together(g_behind, g_ahead, b_ring)
    g_opposite = left(g_behind)
    b_y = over_y(b_ring_late)
    a2_near = join(a2, a2_y)
    near = join(a1_near, a2_near)
    a2_far = over_z(a2_near)
    near_late, g_opposite = together(near, g_opposite)
    near_left, near_right = right(near), left(near_late)
    g_ring = join(g, g_behind, g_ahead, g_opposite)

    b_z, g_ring_out = together(b_z, g_ring)
    g_y, g_z = over_y(g_ring_out), over_z(g_ring_out)
    far = join(a1_far, a2_far)
    near, b_ring, g_ring, b_z = experts([near, b_ring, g_ring, b_z], *matrices)
    far_left, far_right = right(far), left(far)

    near_left, near_right, far, b_y, near, b_ring, g_ring, b_z = together(
        near_left, near_right, far, b_y, near, b_ring, g_ring, b_z
    )
    near_opposite, b_yz = left(near_right), over_z(b_y)
    near_left, near_right, far, b_y = experts([near_left, near_right, far, b_y], *matrices)

    far_left, far_right, g_y, g_z, near_left, near_right, far, b_y = together(
        far_left, far_right, g_y, g_z, near_left, near_right, far, b_y
    )
    far_opposite, g_zy = right(far_left), over_y(g_z)
    far_left, far_right, g_y, g_z = experts([far_left, far_right, g_y, g_z], *matrices)

    near_opposite, far_opposite, b_yz, g_zy, far_left, far_right, g_y, g_z = together(
        near_opposite, far_opposite, b_yz, g_zy, far_left, far_right, g_y, g_z
    )
    near_back, far_back, b_back, g_own = (
        left(near_left), right(far_right), over_y(b_y), over_z(g_ring)
    )
    near_opposite, far_opposite, b_yz, g_zy = experts(
        [near_opposite, far_opposite, b_yz, g_zy], *matrices
    )
    near_opposite, far_opposite, b_yz, g_y, near_back, far_back, b_back, g_own = together(
        near_opposite, far_opposite, b_yz, g_y, near_back, far_back, b_back, g_own
    )
    got = right(near_opposite), left(far_opposite), over_y(b_yz), over_z(g_y)
    near_right, far_left = add(near_right, got[0]), add(far_left, got[1])
    b_ring, g_zy = add(b_ring, b_back), add(g_zy, got[3])
    info, b_yz_back, near_right, far_left, b_ring, g_zy = together(
        info, got[2], near_right, far_left, b_ring, g_zy
    )
    *got, info = together(
        right(near_right), left(far_left), over_z(b_ring), over_y(g_zy), to_next_section(info)
    )

    near, far = (near, near_back, got[0]), (far, far_back, got[1])
    b_terms, g_terms = (b_z, b_yz_back, got[2]), (g_z, g_own, got[3])
    got = sums(
        [take(b_terms, 3, 4), take(g_terms, 2, 4)],
        [take(g_terms, 3, 4), take(b_terms, 2, 4)],
        [take(near, 0, 2)],
        [take(near, 3, 4), take(far, 3, 4)],
    )
    got = together(left(got[0]), right(got[1]), over_z(got[2]), over_y(got[3]))
    ends = sums(
        [take(b_terms, 1, 4) + take(got[:1], 0, 2)],
        [take(g_terms, 1, 4) + take(got[1:2], 0, 2)],
        [take(far, 1, 4) + take(got[2:3], 1, 2)],
        [take(near, 2, 4) + take(got[3:], 0, 2)],
    )
    ends = together(left(ends[0]), right(ends[1]), over_y(ends[2]), over_z(ends[3]))
    own, partner = sums(
        [
            take(far, 0, 4) + take(got[2:3], 0, 2) + take(ends[2:3], 0, 1),
            take(b_terms, 0, 4) + take(got[1:2], 1, 2) + take(ends[:1], 0, 1),
        ],
        [
            take(far, 2, 4) + take(got[3:], 1, 2) + take(ends[3:], 0, 1),
            take(g_terms, 0, 4) + take(got[:1], 1, 2) + take(ends[1:2], 0, 1),
        ],
    )

    own_done, other_done = to_owner(own), to_owner_across(partner)

    def contribution(position, weight, done):
        table = position[:, None] == jnp.arange(CAP, dtype=F32)[None]
        rows = jnp.dot(table.astype(BF16), done, preferred_element_type=F32)
        return weight[:, None] * rows

    mixed = contribution(info[0], info[2], own_done) + contribution(info[1], info[3], other_done)
    return mixed.astype(BF16)[None]


def solution(mesh):
    shape = (2, 2, 2, 2, 4, 2)
    fine = Mesh(mesh.devices.reshape(shape), ("zh", "core", "yh", "yl", "x", "zl"))
    section, ep = ("zh", "core"), ("yh", "yl", "x", "zl")
    rows = P(section, ep, None)
    columns = P(section, None, ep)
    return jax.shard_map(
        body,
        mesh=fine,
        in_specs=(rows, rows, rows, rows, columns, columns, rows),
        out_specs=rows,
        check_vma=False,
    )
```

```python
import jax
import jax.numpy as jnp
from jax import lax
from jax.experimental import pallas as pl
from jax.experimental.pallas import tpu as pltpu
from jax.sharding import Mesh, PartitionSpec as P

CAP = 48
PIECE = 24
F32 = jnp.float32
BF16 = jnp.bfloat16


def shift(value, axis, by):
    n = lax.axis_size(axis)
    return lax.ppermute(value, axis, [(i, (i + by) % n) for i in range(n)])


def right(value):
    return shift(value, "x", 1)


def left(value):
    return shift(value, "x", -1)


def over_y(value):
    return shift(value, "yl", 1)


def over_z(value):
    return shift(value, "zl", 1)


def to_partner(value):
    return lax.ppermute(value, ("yh", "yl"), [(y, 3 - y) for y in range(4)])


def to_next_section(value):
    return lax.ppermute(value, ("zh", "core"), [(s, (s + 1) % 4) for s in range(4)])


def to_owner(value):
    pairs = [(s * 2 + z, (s + 1) % 4 * 2 + 1 - z) for s in range(4) for z in range(2)]
    return lax.ppermute(value, ("zh", "core", "zl"), pairs)


def to_owner_across(value):
    pairs = [
        ((s * 4 + y) * 2 + z, ((s + 1) % 4 * 4 + 3 - y) * 2 + 1 - z)
        for s in range(4)
        for y in range(4)
        for z in range(2)
    ]
    return lax.ppermute(value, ("zh", "core", "yh", "yl", "zl"), pairs)


def together(*values):
    return lax.optimization_barrier(values)


def join(*pieces):
    return jnp.concatenate(pieces)


def add(*terms):
    total = terms[0].astype(F32)
    for term in terms[1:]:
        total = total + term.astype(F32)
    return total.astype(BF16)


def split(rows, count):
    size = rows.shape[0] // count
    return [rows[i * size : (i + 1) * size] for i in range(count)]


def take(arrays, part, parts):
    return [(array, part, array.shape[0] // parts) for array in arrays]


def sums(*wanted):
    pick = lambda array, part, rows: array[part * rows : (part + 1) * rows]
    out = []
    for segments in wanted:
        out.append(join(*(add(*(pick(*term) for term in terms)) for terms in segments)))
    return out


TILE = 1536


def experts_kernel(*refs):
    count = (len(refs) - 6) // 2
    rows, (w_gate, w_up, w_down), rest = refs[:count], refs[count : count + 3], refs[count + 3 :]
    outs, (gate, up, hidden) = rest[:count], rest[count:]
    step = pl.program_id(0)
    half = pl.num_programs(0) // 2

    @pl.when(step < half)
    def _():
        block = jnp.concatenate([r[...] for r in rows])
        gate_part = jnp.dot(block, w_gate[...], preferred_element_type=F32)
        up_part = jnp.dot(block, w_up[...], preferred_element_type=F32)

        @pl.when(step == 0)
        def _():
            gate[...] = gate_part
            up[...] = up_part

        @pl.when(step > 0)
        def _():
            gate[...] += gate_part
            up[...] += up_part

    @pl.when(step >= half)
    def _():
        @pl.when(step == half)
        def _():
            v = gate[...]
            hidden[...] = (v / (1.0 + jnp.exp(-v)) * up[...]).astype(BF16)

        out = jnp.dot(hidden[...], w_down[...], preferred_element_type=F32).astype(BF16)
        start = 0
        for o in outs:
            o[...] = out[start : start + o.shape[0]]
            start += o.shape[0]


def experts(pieces, gate_matrix, up_matrix, down_matrix):
    sizes, width = [p.shape[0] for p in pieces], pieces[0].shape[1]
    units = gate_matrix.shape[1]
    half = width // TILE
    first = lambda i: jnp.minimum(i, half - 1)
    second = lambda i: jnp.maximum(i - half, 0)
    rows_in = [pl.BlockSpec((n, TILE), lambda i: (0, first(i))) for n in sizes]
    rows_out = [pl.BlockSpec((n, TILE), lambda i: (0, second(i))) for n in sizes]
    into = pl.BlockSpec((TILE, units), lambda i: (first(i), 0))
    out_of = pl.BlockSpec((units, TILE), lambda i: (0, second(i)))
    total = sum(sizes)
    return pl.pallas_call(
        experts_kernel,
        grid=(2 * half,),
        in_specs=rows_in + [into, into, out_of],
        out_specs=rows_out,
        out_shape=[jax.ShapeDtypeStruct((n, width), BF16) for n in sizes],
        scratch_shapes=[
            pltpu.VMEM((total, units), F32),
            pltpu.VMEM((total, units), F32),
            pltpu.VMEM((total, units), BF16),
        ],
        compiler_params=pltpu.CompilerParams(
            dimension_semantics=("arbitrary",), vmem_limit_bytes=20 << 20
        ),
        cost_estimate=pl.CostEstimate(
            flops=6 * total * width * units,
            transcendentals=total * units,
            bytes_accessed=6 * width * units + 4 * total * width,
        ),
        name="experts",
    )(*pieces, gate_matrix, up_matrix, down_matrix)


def body(states, expert_ids, gate_values, keep_mask, w_gate, w_up, w_down):
    tokens = states[0]
    ids, gates, keep = expert_ids[0], gate_values[0], keep_mask[0]
    matrices = (w_gate[0], w_up[0], w_down[0])
    mine = lax.axis_index("yh")
    other = 1 - mine

    def slots(expert):
        chosen = (ids == expert) & (keep == 1)
        picked = jnp.any(chosen, axis=1)
        position = jnp.where(picked, jnp.cumsum(picked.astype(jnp.int32)) - 1, -1)
        return position, jnp.sum(jnp.where(chosen, gates, 0.0), axis=1)

    def compact(position, tokens):
        table = position[None] == jnp.arange(CAP, dtype=jnp.int32)[:, None]
        return jnp.dot(table.astype(BF16), tokens, preferred_element_type=F32).astype(BF16)

    (mine_at, mine_weight), (other_at, other_weight) = slots(mine), slots(other)
    info = jnp.stack([mine_at.astype(F32), other_at.astype(F32), mine_weight, other_weight])

    others, tokens = together(compact(other_at, tokens), tokens)
    partner = to_partner(others)
    own = compact(mine_at, tokens)

    a1, b = split(own, 2)
    a1_y, b_behind, b_ahead = over_y(a1), right(b), left(b)
    a1_near = join(a1, a1_y)
    a1_far, b_opposite = over_z(a1_near), right(b_behind)
    partner, b_ahead, b_opposite = together(partner, b_ahead, b_opposite)
    b_ring = join(b, b_behind, b_ahead, b_opposite)
    b_y = over_y(b_ring)

    a2, g = split(partner, 2)
    a2_z, g_behind, g_ahead = over_z(a2), left(g), right(g)
    g_behind, g_ahead, b_ring_late = together(g_behind, g_ahead, b_ring)
    g_opposite = left(g_behind)
    a2_near = join(a2, a2_z)
    near = join(a1_near, a2_near)
    a2_far, b_z = over_y(a2_near), over_z(b_ring_late)
    near_late, g_opposite = together(near, g_opposite)
    near_left, near_right = right(near), left(near_late)
    g_ring = join(g, g_behind, g_ahead, g_opposite)

    g_ring_sent = g_ring
    near, b_ring, g_ring = experts([near, b_ring, g_ring], *matrices)
    b_y, near, g_ring_y = together(b_y, near, g_ring_sent)
    b_z, g_ring_z = together(b_z, g_ring_sent)
    g_y, g_z = over_y(g_ring_y), over_z(g_ring_z)
    a2_far, near_left, b_z = together(a2_far, near_left, b_z)
    far = join(a1_far, a2_far)
    far_left, far_right = right(far), left(far)

    near_right_sent, b_y_sent = near_right, b_y
    near_left, near_right, far, b_y, b_z = experts(
        [near_left, near_right, far, b_y, b_z], *matrices
    )
    near_right_sent, b_y_sent, far = together(near_right_sent, b_y_sent, far)
    near_opposite, b_yz = left(near_right_sent), over_z(b_y_sent)
    far_opposite, g_zy = right(far_left), over_y(g_z)
    far_left, far_right, g_y, g_z, far = together(far_left, far_right, g_y, g_z, far)
    far_left, far_right, g_y, g_z = experts([far_left, far_right, g_y, g_z], *matrices)

    near_opposite, far_opposite, b_yz, g_zy, far_left, far_right, g_y, g_z = together(
        near_opposite, far_opposite, b_yz, g_zy, far_left, far_right, g_y, g_z
    )
    near_back, far_back, b_back, g_own = (
        left(near_left), right(far_right), over_y(b_y), over_z(g_ring)
    )
    near_opposite, far_opposite, b_yz, g_zy = experts(
        [near_opposite, far_opposite, b_yz, g_zy], *matrices
    )
    near_opposite, far_opposite, b_yz, g_y, near_back, far_back, b_back, g_own = together(
        near_opposite, far_opposite, b_yz, g_y, near_back, far_back, b_back, g_own
    )
    got = right(near_opposite), left(far_opposite), over_y(b_yz), over_z(g_y)
    near_right, far_left = add(near_right, got[0]), add(far_left, got[1])
    b_ring, g_zy = add(b_ring, b_back), add(g_zy, got[3])
    info, b_yz_back, near_right, far_left, b_ring, g_zy = together(
        info, got[2], near_right, far_left, b_ring, g_zy
    )
    *got, info = together(
        right(near_right), left(far_left), over_z(b_ring), over_y(g_zy), to_next_section(info)
    )

    near, far = (near, near_back, got[0]), (far, far_back, got[1])
    b_terms, g_terms = (b_z, b_yz_back, got[2]), (g_z, g_own, got[3])
    got = sums(
        [take(b_terms, 3, 4), take(g_terms, 2, 4)],
        [take(g_terms, 3, 4), take(b_terms, 2, 4)],
        [take(near, 0, 2)],
        [take(far, 1, 2)],
    )
    got = together(left(got[0]), right(got[1]), over_z(got[2]), over_y(got[3]))
    a1_terms = take(far, 0, 4), take(far, 1, 4)
    a2_terms = take(near, 2, 4), take(near, 3, 4)
    ends = sums(
        [take(b_terms, 1, 4) + take(got[:1], 0, 2)],
        [take(g_terms, 1, 4) + take(got[1:2], 0, 2)],
        [a1_terms[1] + take(got[2:3], 1, 2)],
        [a2_terms[0] + take(got[3:], 0, 2)],
    )
    ends = together(left(ends[0]), right(ends[1]), over_y(ends[2]), over_z(ends[3]))
    own, partner = sums(
        [
            a1_terms[0] + take(got[2:3], 0, 2) + take(ends[2:3], 0, 1),
            take(b_terms, 0, 4) + take(got[1:2], 1, 2) + take(ends[:1], 0, 1),
        ],
        [
            a2_terms[1] + take(got[3:], 1, 2) + take(ends[3:], 0, 1),
            take(g_terms, 0, 4) + take(got[:1], 1, 2) + take(ends[1:2], 0, 1),
        ],
    )

    own_done, other_done = to_owner(own), to_owner_across(partner)

    def contribution(position, weight, done):
        table = position[:, None] == jnp.arange(CAP, dtype=F32)[None]
        rows = jnp.dot(table.astype(BF16), done, preferred_element_type=F32)
        return weight[:, None] * rows

    mixed = contribution(info[0], info[2], own_done) + contribution(info[1], info[3], other_done)
    return mixed.astype(BF16)[None]


def solution(mesh):
    shape = (2, 2, 2, 2, 4, 2)
    fine = Mesh(mesh.devices.reshape(shape), ("zh", "core", "yh", "yl", "x", "zl"))
    section, ep = ("zh", "core"), ("yh", "yl", "x", "zl")
    rows = P(section, ep, None)
    columns = P(section, None, ep)
    return jax.shard_map(
        body,
        mesh=fine,
        in_specs=(rows, rows, rows, rows, columns, columns, rows),
        out_specs=rows,
        check_vma=False,
    )
```

```python
import jax
import jax.numpy as jnp
from jax import lax
from jax.experimental import pallas as pl
from jax.experimental.pallas import tpu as pltpu
from jax.sharding import Mesh, PartitionSpec as P

CAP = 48
PIECE = 24
F32 = jnp.float32
BF16 = jnp.bfloat16


def shift(value, axis, by):
    n = lax.axis_size(axis)
    return lax.ppermute(value, axis, [(i, (i + by) % n) for i in range(n)])


def right(value):
    return shift(value, "x", 1)


def left(value):
    return shift(value, "x", -1)


def over_y(value):
    return shift(value, "yl", 1)


def over_z(value):
    return shift(value, "zl", 1)


def to_partner(value):
    return lax.ppermute(value, ("yh", "yl"), [(y, 3 - y) for y in range(4)])


def to_next_section(value):
    return lax.ppermute(value, ("zh", "core"), [(s, (s + 1) % 4) for s in range(4)])


def to_owner(value):
    pairs = [(s * 2 + z, (s + 1) % 4 * 2 + 1 - z) for s in range(4) for z in range(2)]
    return lax.ppermute(value, ("zh", "core", "zl"), pairs)


def to_owner_across(value):
    pairs = [
        ((s * 4 + y) * 2 + z, ((s + 1) % 4 * 4 + 3 - y) * 2 + 1 - z)
        for s in range(4)
        for y in range(4)
        for z in range(2)
    ]
    return lax.ppermute(value, ("zh", "core", "yh", "yl", "zl"), pairs)


def together(*values):
    return lax.optimization_barrier(values)


def join(*pieces):
    return jnp.concatenate(pieces)


def add(*terms):
    total = terms[0].astype(F32)
    for term in terms[1:]:
        total = total + term.astype(F32)
    return total.astype(BF16)


def split(rows, count):
    size = rows.shape[0] // count
    return [rows[i * size : (i + 1) * size] for i in range(count)]


def take(arrays, part, parts):
    return [(array, part, array.shape[0] // parts) for array in arrays]


def sums(*wanted):
    pick = lambda array, part, rows: array[part * rows : (part + 1) * rows]
    out = []
    for segments in wanted:
        out.append(join(*(add(*(pick(*term) for term in terms)) for terms in segments)))
    return out


TILE = 1536


def experts_kernel(*refs):
    count = (len(refs) - 6) // 2
    rows, (w_gate, w_up, w_down), rest = refs[:count], refs[count : count + 3], refs[count + 3 :]
    outs, (gate, up, hidden) = rest[:count], rest[count:]
    step = pl.program_id(0)
    half = pl.num_programs(0) // 2

    @pl.when(step < half)
    def _():
        block = jnp.concatenate([r[...] for r in rows])
        gate_part = jnp.dot(block, w_gate[...], preferred_element_type=F32)
        up_part = jnp.dot(block, w_up[...], preferred_element_type=F32)

        @pl.when(step == 0)
        def _():
            gate[...] = gate_part
            up[...] = up_part

        @pl.when(step > 0)
        def _():
            gate[...] += gate_part
            up[...] += up_part

    @pl.when(step >= half)
    def _():
        @pl.when(step == half)
        def _():
            v = gate[...]
            hidden[...] = (v / (1.0 + jnp.exp(-v)) * up[...]).astype(BF16)

        out = jnp.dot(hidden[...], w_down[...], preferred_element_type=F32).astype(BF16)
        start = 0
        for o in outs:
            o[...] = out[start : start + o.shape[0]]
            start += o.shape[0]


def experts(pieces, gate_matrix, up_matrix, down_matrix):
    sizes, width = [p.shape[0] for p in pieces], pieces[0].shape[1]
    units = gate_matrix.shape[1]
    half = width // TILE
    first = lambda i: jnp.minimum(i, half - 1)
    second = lambda i: jnp.maximum(i - half, 0)
    rows_in = [pl.BlockSpec((n, TILE), lambda i: (0, first(i))) for n in sizes]
    rows_out = [pl.BlockSpec((n, TILE), lambda i: (0, second(i))) for n in sizes]
    into = pl.BlockSpec((TILE, units), lambda i: (first(i), 0))
    out_of = pl.BlockSpec((units, TILE), lambda i: (0, second(i)))
    total = sum(sizes)
    return pl.pallas_call(
        experts_kernel,
        grid=(2 * half,),
        in_specs=rows_in + [into, into, out_of],
        out_specs=rows_out,
        out_shape=[jax.ShapeDtypeStruct((n, width), BF16) for n in sizes],
        scratch_shapes=[
            pltpu.VMEM((total, units), F32),
            pltpu.VMEM((total, units), F32),
            pltpu.VMEM((total, units), BF16),
        ],
        compiler_params=pltpu.CompilerParams(
            dimension_semantics=("arbitrary",), vmem_limit_bytes=20 << 20
        ),
        cost_estimate=pl.CostEstimate(
            flops=6 * total * width * units,
            transcendentals=total * units,
            bytes_accessed=6 * width * units + 4 * total * width,
        ),
        name="experts",
    )(*pieces, gate_matrix, up_matrix, down_matrix)


def body(states, expert_ids, gate_values, keep_mask, w_gate, w_up, w_down):
    tokens = states[0]
    ids, gates, keep = expert_ids[0], gate_values[0], keep_mask[0]
    matrices = (w_gate[0], w_up[0], w_down[0])
    mine = lax.axis_index("yh")
    other = 1 - mine

    def slots(expert):
        chosen = (ids == expert) & (keep == 1)
        picked = jnp.any(chosen, axis=1)
        position = jnp.where(picked, jnp.cumsum(picked.astype(jnp.int32)) - 1, -1)
        return position, jnp.sum(jnp.where(chosen, gates, 0.0), axis=1)

    def compact(position, tokens):
        table = position[None] == jnp.arange(CAP, dtype=jnp.int32)[:, None]
        return jnp.dot(table.astype(BF16), tokens, preferred_element_type=F32).astype(BF16)

    (mine_at, mine_weight), (other_at, other_weight) = slots(mine), slots(other)
    info = jnp.stack([mine_at.astype(F32), other_at.astype(F32), mine_weight, other_weight])

    others, tokens = together(compact(other_at, tokens), tokens)
    partner = to_partner(others)
    own = compact(mine_at, tokens)

    a1, b = split(own, 2)
    partner, a1_y, b_behind, b_ahead = together(partner, over_y(a1), right(b), left(b))

    a2, g = split(partner, 2)
    b_opposite, a2_z, g_behind, g_ahead = right(b_behind), over_z(a2), left(g), right(g)
    b_opposite, a1, a1_y = together(b_opposite, a1, a1_y)
    a1_near = join(a1, a1_y)
    a1_far = over_z(a1_near)
    b_ring = join(b, b_behind, b_ahead, b_opposite)
    g_behind, g_ahead = together(g_behind, g_ahead)
    g_opposite = left(g_behind)
    a2_near = join(a2, a2_z)
    a2_far = over_y(a2_near)
    near = join(a1_near, a2_near)
    near_late, g_opposite, b_ring = together(near, g_opposite, b_ring)
    near_left, near_right = right(near), left(near_late)
    b_y = over_y(b_ring)
    a1_far, b_ring = together(a1_far, b_ring)
    b_z = over_z(b_ring)
    g_ring = join(g, g_behind, g_ahead, g_opposite)

    g_ring_sent = g_ring
    near, b_ring, g_ring = experts([near, b_ring, g_ring], *matrices)
    b_y, g_ring_y = together(b_y, g_ring_sent)
    b_z, g_ring_z = together(b_z, g_ring_sent)
    g_y, g_z = over_y(g_ring_y), over_z(g_ring_z)
    a2_far, near_left, b_ring = together(a2_far, near_left, b_ring)
    far = join(a1_far, a2_far)
    far_left, far_right = right(far), left(far)

    near_right_sent, b_y_sent = near_right, b_y
    near_left, near_right, far, b_y, b_z = experts(
        [near_left, near_right, far, b_y, b_z], *matrices
    )
    near_right_sent, b_y_sent, far = together(near_right_sent, b_y_sent, far)
    near_opposite, b_yz = left(near_right_sent), over_z(b_y_sent)
    far_opposite, g_zy = right(far_left), over_y(g_z)
    far_left, far_right, g_y, g_z, far = together(far_left, far_right, g_y, g_z, far)
    far_left, far_right, g_y, g_z = experts([far_left, far_right, g_y, g_z], *matrices)

    near_opposite, far_opposite, b_yz, g_zy, far_left, far_right, g_y, g_z = together(
        near_opposite, far_opposite, b_yz, g_zy, far_left, far_right, g_y, g_z
    )
    near_back, far_back, b_back, g_own = (
        left(near_left), right(far_right), over_y(b_y), over_z(g_ring)
    )
    near_opposite, far_opposite, b_yz, g_zy = experts(
        [near_opposite, far_opposite, b_yz, g_zy], *matrices
    )
    near_opposite, far_opposite, b_yz, g_y, near_back, far_back, b_back, g_own = together(
        near_opposite, far_opposite, b_yz, g_y, near_back, far_back, b_back, g_own
    )
    got = right(near_opposite), left(far_opposite), over_y(b_yz), over_z(g_y)
    near_right, far_left = add(near_right, got[0]), add(far_left, got[1])
    b_ring, g_zy = add(b_ring, b_back), add(g_zy, got[3])
    info, b_yz_back, near_right, far_left, b_ring, g_zy = together(
        info, got[2], near_right, far_left, b_ring, g_zy
    )
    *got, info = together(
        right(near_right), left(far_left), over_z(b_ring), over_y(g_zy), to_next_section(info)
    )

    near, far = (near, near_back, got[0]), (far, far_back, got[1])
    b_terms, g_terms = (b_z, b_yz_back, got[2]), (g_z, g_own, got[3])
    got = sums(
        [take(b_terms, 3, 4), take(g_terms, 2, 4)],
        [take(g_terms, 3, 4), take(b_terms, 2, 4)],
        [take(near, 0, 2)],
        [take(far, 1, 2)],
    )
    got = together(left(got[0]), right(got[1]), over_z(got[2]), over_y(got[3]))
    a1_terms = take(far, 0, 4), take(far, 1, 4)
    a2_terms = take(near, 2, 4), take(near, 3, 4)
    ends = sums(
        [take(b_terms, 1, 4) + take(got[:1], 0, 2)],
        [take(g_terms, 1, 4) + take(got[1:2], 0, 2)],
        [a1_terms[1] + take(got[2:3], 1, 2)],
        [a2_terms[0] + take(got[3:], 0, 2)],
    )
    ends = left(ends[0]), right(ends[1]), over_y(ends[2]), over_z(ends[3])
    own, partner = sums(
        [
            a1_terms[0] + take(got[2:3], 0, 2) + take(ends[2:3], 0, 1),
            take(b_terms, 0, 4) + take(got[1:2], 1, 2) + take(ends[:1], 0, 1),
        ],
        [
            a2_terms[1] + take(got[3:], 1, 2) + take(ends[3:], 0, 1),
            take(g_terms, 0, 4) + take(got[:1], 1, 2) + take(ends[1:2], 0, 1),
        ],
    )

    own_done, other_done = to_owner(own), to_owner_across(partner)

    def contribution(position, weight, done):
        table = position[:, None] == jnp.arange(CAP, dtype=F32)[None]
        rows = jnp.dot(table.astype(BF16), done, preferred_element_type=F32)
        return weight[:, None] * rows

    mixed = contribution(info[0], info[2], own_done) + contribution(info[1], info[3], other_done)
    return mixed.astype(BF16)[None]


def solution(mesh):
    shape = (2, 2, 2, 2, 4, 2)
    fine = Mesh(mesh.devices.reshape(shape), ("zh", "core", "yh", "yl", "x", "zl"))
    section, ep = ("zh", "core"), ("yh", "yl", "x", "zl")
    rows = P(section, ep, None)
    columns = P(section, None, ep)
    return jax.shard_map(
        body,
        mesh=fine,
        in_specs=(rows, rows, rows, rows, columns, columns, rows),
        out_specs=rows,
        check_vma=False,
    )
```

```python
import jax
import jax.numpy as jnp
from jax import lax
from jax.experimental import pallas as pl
from jax.experimental.pallas import tpu as pltpu
from jax.sharding import Mesh, PartitionSpec as P

CAP = 48
PIECE = 24
F32 = jnp.float32
BF16 = jnp.bfloat16


def shift(value, axis, by):
    n = lax.axis_size(axis)
    return lax.ppermute(value, axis, [(i, (i + by) % n) for i in range(n)])


def right(value):
    return shift(value, "x", 1)


def left(value):
    return shift(value, "x", -1)


def over_y(value):
    return shift(value, "yl", 1)


def over_z(value):
    return shift(value, "zl", 1)


def to_partner(value):
    return lax.ppermute(value, ("yh", "yl"), [(y, 3 - y) for y in range(4)])


def to_next_section(value):
    return lax.ppermute(value, ("zh", "core"), [(s, (s + 1) % 4) for s in range(4)])


def to_owner(value):
    pairs = [(s * 2 + z, (s + 1) % 4 * 2 + 1 - z) for s in range(4) for z in range(2)]
    return lax.ppermute(value, ("zh", "core", "zl"), pairs)


def to_owner_across(value):
    pairs = [
        ((s * 4 + y) * 2 + z, ((s + 1) % 4 * 4 + 3 - y) * 2 + 1 - z)
        for s in range(4)
        for y in range(4)
        for z in range(2)
    ]
    return lax.ppermute(value, ("zh", "core", "yh", "yl", "zl"), pairs)


def together(*values):
    return lax.optimization_barrier(values)


def join(*pieces):
    return jnp.concatenate(pieces)


def add(*terms):
    total = terms[0].astype(F32)
    for term in terms[1:]:
        total = total + term.astype(F32)
    return total.astype(BF16)


def split(rows, count):
    size = rows.shape[0] // count
    return [rows[i * size : (i + 1) * size] for i in range(count)]


def take(arrays, part, parts):
    return [(array, part, array.shape[0] // parts) for array in arrays]


def sums(*wanted):
    pick = lambda array, part, rows: array[part * rows : (part + 1) * rows]
    out = []
    for segments in wanted:
        out.append(join(*(add(*(pick(*term) for term in terms)) for terms in segments)))
    return out


TILE = 1536


def experts_kernel(*refs):
    count = (len(refs) - 6) // 2
    rows, (w_gate, w_up, w_down), rest = refs[:count], refs[count : count + 3], refs[count + 3 :]
    outs, (gate, up, hidden) = rest[:count], rest[count:]
    step = pl.program_id(0)
    half = pl.num_programs(0) // 2

    @pl.when(step < half)
    def _():
        block = jnp.concatenate([r[...] for r in rows])
        gate_part = jnp.dot(block, w_gate[...], preferred_element_type=F32)
        up_part = jnp.dot(block, w_up[...], preferred_element_type=F32)

        @pl.when(step == 0)
        def _():
            gate[...] = gate_part
            up[...] = up_part

        @pl.when(step > 0)
        def _():
            gate[...] += gate_part
            up[...] += up_part

    @pl.when(step >= half)
    def _():
        @pl.when(step == half)
        def _():
            v = gate[...]
            hidden[...] = (v / (1.0 + jnp.exp(-v)) * up[...]).astype(BF16)

        out = jnp.dot(hidden[...], w_down[...], preferred_element_type=F32).astype(BF16)
        start = 0
        for o in outs:
            o[...] = out[start : start + o.shape[0]]
            start += o.shape[0]


def experts(pieces, gate_matrix, up_matrix, down_matrix):
    sizes, width = [p.shape[0] for p in pieces], pieces[0].shape[1]
    units = gate_matrix.shape[1]
    half = width // TILE
    first = lambda i: jnp.minimum(i, half - 1)
    second = lambda i: jnp.maximum(i - half, 0)
    rows_in = [pl.BlockSpec((n, TILE), lambda i: (0, first(i))) for n in sizes]
    rows_out = [pl.BlockSpec((n, TILE), lambda i: (0, second(i))) for n in sizes]
    into = pl.BlockSpec((TILE, units), lambda i: (first(i), 0))
    out_of = pl.BlockSpec((units, TILE), lambda i: (0, second(i)))
    total = sum(sizes)
    return pl.pallas_call(
        experts_kernel,
        grid=(2 * half,),
        in_specs=rows_in + [into, into, out_of],
        out_specs=rows_out,
        out_shape=[jax.ShapeDtypeStruct((n, width), BF16) for n in sizes],
        scratch_shapes=[
            pltpu.VMEM((total, units), F32),
            pltpu.VMEM((total, units), F32),
            pltpu.VMEM((total, units), BF16),
        ],
        compiler_params=pltpu.CompilerParams(
            dimension_semantics=("arbitrary",), vmem_limit_bytes=20 << 20
        ),
        cost_estimate=pl.CostEstimate(
            flops=6 * total * width * units,
            transcendentals=total * units,
            bytes_accessed=6 * width * units + 4 * total * width,
        ),
        name="experts",
    )(*pieces, gate_matrix, up_matrix, down_matrix)


def body(states, expert_ids, gate_values, keep_mask, w_gate, w_up, w_down):
    tokens = states[0]
    ids, gates, keep = expert_ids[0], gate_values[0], keep_mask[0]
    matrices = (w_gate[0], w_up[0], w_down[0])
    mine = lax.axis_index("yh")
    other = 1 - mine

    def slots(expert):
        chosen = (ids == expert) & (keep == 1)
        picked = jnp.any(chosen, axis=1)
        position = jnp.where(picked, jnp.cumsum(picked.astype(jnp.int32)) - 1, -1)
        return position, jnp.sum(jnp.where(chosen, gates, 0.0), axis=1)

    def compact(position, tokens):
        table = position[None] == jnp.arange(CAP, dtype=jnp.int32)[:, None]
        return jnp.dot(table.astype(BF16), tokens, preferred_element_type=F32).astype(BF16)

    (mine_at, mine_weight), (other_at, other_weight) = slots(mine), slots(other)
    info = jnp.stack([mine_at.astype(F32), other_at.astype(F32), mine_weight, other_weight])

    others, tokens = together(compact(other_at, tokens), tokens)
    partner = to_partner(others)
    own = compact(mine_at, tokens)

    a1, b = split(own, 2)
    a1_y, b_behind, b_ahead = over_y(a1), right(b), left(b)
    b_opposite = right(b_behind)
    b_ring = join(b, b_behind, b_ahead, b_opposite)
    b_y = over_y(b_ring)
    partner, a1_y = together(partner, a1_y)
    a1_near = join(a1, a1_y)
    a1_far = over_z(a1_near)

    a2, g = split(partner, 2)
    a2_z, g_behind, g_ahead = over_z(a2), left(g), right(g)
    a2_z, g_behind = together(a2_z, g_behind)
    g_opposite = left(g_behind)
    a1_far, b_ring_late = together(a1_far, b_ring)
    a2_near = join(a2, a2_z)
    near = join(a1_near, a2_near)
    a2_far, b_z = over_y(a2_near), over_z(b_ring_late)
    near, g_opposite, g_ahead = together(near, g_opposite, g_ahead)
    near_left, near_right = right(near), left(near)
    g_ring = join(g, g_behind, g_ahead, g_opposite)

    g_ring_sent = g_ring
    near, b_ring, g_ring = experts([near, b_ring, g_ring], *matrices)
    b_y, g_ring_y = together(b_y, g_ring_sent)
    b_z, g_ring_z = together(b_z, g_ring_sent)
    g_y, g_z = over_y(g_ring_y), over_z(g_ring_z)
    a2_far, near_left, b_ring = together(a2_far, near_left, b_ring)
    far = join(a1_far, a2_far)
    far_left, far_right = right(far), left(far)

    near_right_sent, b_y_sent = near_right, b_y
    near_left, near_right, far, b_y, b_z = experts(
        [near_left, near_right, far, b_y, b_z], *matrices
    )
    near_right_sent, b_y_sent, far = together(near_right_sent, b_y_sent, far)
    near_opposite, b_yz = left(near_right_sent), over_z(b_y_sent)
    far_opposite, g_zy = right(far_left), over_y(g_z)
    far_left, far_right, g_y, g_z, far = together(far_left, far_right, g_y, g_z, far)
    far_left, far_right, g_y, g_z = experts([far_left, far_right, g_y, g_z], *matrices)

    near_opposite, far_opposite, b_yz, g_zy, far_left, far_right, g_y, g_z = together(
        near_opposite, far_opposite, b_yz, g_zy, far_left, far_right, g_y, g_z
    )
    near_back, far_back, b_back, g_own = (
        left(near_left), right(far_right), over_y(b_y), over_z(g_ring)
    )
    near_opposite, far_opposite, b_yz, g_zy = experts(
        [near_opposite, far_opposite, b_yz, g_zy], *matrices
    )
    near_opposite, far_opposite, b_yz, g_y, near_back, far_back, b_back, g_own = together(
        near_opposite, far_opposite, b_yz, g_y, near_back, far_back, b_back, g_own
    )
    got = right(near_opposite), left(far_opposite), over_y(b_yz), over_z(g_y)
    near_right, far_left = add(near_right, got[0]), add(far_left, got[1])
    b_ring, g_zy = add(b_ring, b_back), add(g_zy, got[3])
    info, b_yz_back, near_right, far_left, b_ring, g_zy = together(
        info, got[2], near_right, far_left, b_ring, g_zy
    )
    *got, info = together(
        right(near_right), left(far_left), over_z(b_ring), over_y(g_zy), to_next_section(info)
    )

    near, far = (near, near_back, got[0]), (far, far_back, got[1])
    b_terms, g_terms = (b_z, b_yz_back, got[2]), (g_z, g_own, got[3])
    got = sums(
        [take(b_terms, 3, 4), take(g_terms, 2, 4)],
        [take(g_terms, 3, 4), take(b_terms, 2, 4)],
        [take(near, 0, 2)],
        [take(far, 1, 2)],
    )
    got = together(left(got[0]), right(got[1]), over_z(got[2]), over_y(got[3]))
    a1_terms = take(far, 0, 4), take(far, 1, 4)
    a2_terms = take(near, 2, 4), take(near, 3, 4)
    ends = sums(
        [take(b_terms, 1, 4) + take(got[:1], 0, 2)],
        [take(g_terms, 1, 4) + take(got[1:2], 0, 2)],
        [a1_terms[1] + take(got[2:3], 1, 2)],
        [a2_terms[0] + take(got[3:], 0, 2)],
    )
    ends = together(left(ends[0]), right(ends[1]), over_y(ends[2]), over_z(ends[3]))
    own, partner = sums(
        [
            a1_terms[0] + take(got[2:3], 0, 2) + take(ends[2:3], 0, 1),
            take(b_terms, 0, 4) + take(got[1:2], 1, 2) + take(ends[:1], 0, 1),
        ],
        [
            a2_terms[1] + take(got[3:], 1, 2) + take(ends[3:], 0, 1),
            take(g_terms, 0, 4) + take(got[:1], 1, 2) + take(ends[1:2], 0, 1),
        ],
    )

    own_done, other_done = to_owner(own), to_owner_across(partner)

    def contribution(position, weight, done):
        table = position[:, None] == jnp.arange(CAP, dtype=F32)[None]
        rows = jnp.dot(table.astype(BF16), done, preferred_element_type=F32)
        return weight[:, None] * rows

    mixed = contribution(info[0], info[2], own_done) + contribution(info[1], info[3], other_done)
    return mixed.astype(BF16)[None]


def solution(mesh):
    shape = (2, 2, 2, 2, 4, 2)
    fine = Mesh(mesh.devices.reshape(shape), ("zh", "core", "yh", "yl", "x", "zl"))
    section, ep = ("zh", "core"), ("yh", "yl", "x", "zl")
    rows = P(section, ep, None)
    columns = P(section, None, ep)
    return jax.shard_map(
        body,
        mesh=fine,
        in_specs=(rows, rows, rows, rows, columns, columns, rows),
        out_specs=rows,
        check_vma=False,
    )
```

```python
import jax
import jax.numpy as jnp
from jax import lax
from jax.experimental import pallas as pl
from jax.experimental.pallas import tpu as pltpu
from jax.sharding import Mesh, PartitionSpec as P

CAP = 48
PIECE = 24
F32 = jnp.float32
BF16 = jnp.bfloat16


def shift(value, axis, by):
    n = lax.axis_size(axis)
    return lax.ppermute(value, axis, [(i, (i + by) % n) for i in range(n)])


def right(value):
    return shift(value, "x", 1)


def left(value):
    return shift(value, "x", -1)


def over_y(value):
    return shift(value, "yl", 1)


def over_z(value):
    return shift(value, "zl", 1)


def to_partner(value):
    return lax.ppermute(value, ("yh", "yl"), [(y, 3 - y) for y in range(4)])


def to_next_section(value):
    return lax.ppermute(value, ("zh", "core"), [(s, (s + 1) % 4) for s in range(4)])


def to_owner(value):
    pairs = [(s * 2 + z, (s + 1) % 4 * 2 + 1 - z) for s in range(4) for z in range(2)]
    return lax.ppermute(value, ("zh", "core", "zl"), pairs)


def to_owner_across(value):
    pairs = [
        ((s * 4 + y) * 2 + z, ((s + 1) % 4 * 4 + 3 - y) * 2 + 1 - z)
        for s in range(4)
        for y in range(4)
        for z in range(2)
    ]
    return lax.ppermute(value, ("zh", "core", "yh", "yl", "zl"), pairs)


def together(*values):
    return lax.optimization_barrier(values)


def join(*pieces):
    return jnp.concatenate(pieces)


def add(*terms):
    total = terms[0].astype(F32)
    for term in terms[1:]:
        total = total + term.astype(F32)
    return total.astype(BF16)


def split(rows, count):
    size = rows.shape[0] // count
    return [rows[i * size : (i + 1) * size] for i in range(count)]


def take(arrays, part, parts):
    return [(array, part, array.shape[0] // parts) for array in arrays]


def sums(*wanted):
    pick = lambda array, part, rows: array[part * rows : (part + 1) * rows]
    out = []
    for segments in wanted:
        out.append(join(*(add(*(pick(*term) for term in terms)) for terms in segments)))
    return out


TILE = 1536


def experts_kernel(*refs):
    count = (len(refs) - 6) // 2
    rows, (w_gate, w_up, w_down), rest = refs[:count], refs[count : count + 3], refs[count + 3 :]
    outs, (gate, up, hidden) = rest[:count], rest[count:]
    step = pl.program_id(0)
    half = pl.num_programs(0) // 2

    @pl.when(step < half)
    def _():
        block = jnp.concatenate([r[...] for r in rows])
        gate_part = jnp.dot(block, w_gate[...], preferred_element_type=F32)
        up_part = jnp.dot(block, w_up[...], preferred_element_type=F32)

        @pl.when(step == 0)
        def _():
            gate[...] = gate_part
            up[...] = up_part

        @pl.when(step > 0)
        def _():
            gate[...] += gate_part
            up[...] += up_part

    @pl.when(step >= half)
    def _():
        @pl.when(step == half)
        def _():
            v = gate[...]
            hidden[...] = (v / (1.0 + jnp.exp(-v)) * up[...]).astype(BF16)

        out = jnp.dot(hidden[...], w_down[...], preferred_element_type=F32).astype(BF16)
        start = 0
        for o in outs:
            o[...] = out[start : start + o.shape[0]]
            start += o.shape[0]


def experts(pieces, gate_matrix, up_matrix, down_matrix):
    sizes, width = [p.shape[0] for p in pieces], pieces[0].shape[1]
    units = gate_matrix.shape[1]
    half = width // TILE
    first = lambda i: jnp.minimum(i, half - 1)
    second = lambda i: jnp.maximum(i - half, 0)
    rows_in = [pl.BlockSpec((n, TILE), lambda i: (0, first(i))) for n in sizes]
    rows_out = [pl.BlockSpec((n, TILE), lambda i: (0, second(i))) for n in sizes]
    into = pl.BlockSpec((TILE, units), lambda i: (first(i), 0))
    out_of = pl.BlockSpec((units, TILE), lambda i: (0, second(i)))
    total = sum(sizes)
    return pl.pallas_call(
        experts_kernel,
        grid=(2 * half,),
        in_specs=rows_in + [into, into, out_of],
        out_specs=rows_out,
        out_shape=[jax.ShapeDtypeStruct((n, width), BF16) for n in sizes],
        scratch_shapes=[
            pltpu.VMEM((total, units), F32),
            pltpu.VMEM((total, units), F32),
            pltpu.VMEM((total, units), BF16),
        ],
        compiler_params=pltpu.CompilerParams(
            dimension_semantics=("arbitrary",), vmem_limit_bytes=18 << 20
        ),
        cost_estimate=pl.CostEstimate(
            flops=6 * total * width * units,
            transcendentals=total * units,
            bytes_accessed=6 * width * units + 4 * total * width,
        ),
        name="experts",
    )(*pieces, gate_matrix, up_matrix, down_matrix)


def body(states, expert_ids, gate_values, keep_mask, w_gate, w_up, w_down):
    tokens = states[0]
    ids, gates, keep = expert_ids[0], gate_values[0], keep_mask[0]
    matrices = (w_gate[0], w_up[0], w_down[0])
    mine = lax.axis_index("yh")
    other = 1 - mine

    def slots(expert):
        chosen = (ids == expert) & (keep == 1)
        picked = jnp.any(chosen, axis=1)
        position = jnp.where(picked, jnp.cumsum(picked.astype(jnp.int32)) - 1, -1)
        return position, jnp.sum(jnp.where(chosen, gates, 0.0), axis=1)

    def compact(position, tokens):
        table = position[None] == jnp.arange(CAP, dtype=jnp.int32)[:, None]
        return jnp.dot(table.astype(BF16), tokens, preferred_element_type=F32).astype(BF16)

    (mine_at, mine_weight), (other_at, other_weight) = slots(mine), slots(other)
    info = jnp.stack([mine_at.astype(F32), other_at.astype(F32), mine_weight, other_weight])

    others, tokens = together(compact(other_at, tokens), tokens)
    partner = to_partner(others)
    own = compact(mine_at, tokens)

    a1, b = split(own, 2)
    a1_y, b_behind, b_ahead = over_y(a1), right(b), left(b)
    a1_near = join(a1, a1_y)
    b_opposite = right(b_behind)
    b_ring = join(b, b_behind, b_ahead, b_opposite)
    b_y = over_y(b_ring)

    a2, g = split(partner, 2)
    a2_z, g_behind, g_ahead = over_z(a2), left(g), right(g)
    g_behind, g_ahead, b_ring_late, a1_near_late = together(g_behind, g_ahead, b_ring, a1_near)
    g_opposite = left(g_behind)
    a1_far = over_z(a1_near_late)
    a2_near = join(a2, a2_z)
    near = join(a1_near, a2_near)
    a1_far, b_ring_late = together(a1_far, b_ring_late)
    a2_far, b_z = over_y(a2_near), over_z(b_ring_late)
    near_late, g_opposite = together(near, g_opposite)
    near_left, near_right = right(near), left(near_late)
    g_ring = join(g, g_behind, g_ahead, g_opposite)

    b_y, g_ring_out = together(b_y, g_ring)
    g_y, g_z = over_y(g_ring_out), over_z(g_ring_out)
    far = join(a1_far, a2_far)
    b_y_sent = b_y
    near, b_ring, g_ring, b_y = experts([near, b_ring, g_ring, b_y], *matrices)
    far_left, far_right = right(far), left(far)

    near_left, near_right, far, b_z, near, b_ring, g_ring, b_y, b_y_sent = together(
        near_left, near_right, far, b_z, near, b_ring, g_ring, b_y, b_y_sent
    )
    near_opposite, b_yz = left(near_right), over_z(b_y_sent)
    near_left, near_right, far, b_z = experts([near_left, near_right, far, b_z], *matrices)

    far_left, far_right, g_y, g_z, near_left, near_right, far, b_z = together(
        far_left, far_right, g_y, g_z, near_left, near_right, far, b_z
    )
    far_opposite, g_zy = right(far_left), over_y(g_z)
    far_left, far_right, g_y, g_z = experts([far_left, far_right, g_y, g_z], *matrices)

    near_opposite, far_opposite, b_yz, g_zy, far_left, far_right, g_y, g_z = together(
        near_opposite, far_opposite, b_yz, g_zy, far_left, far_right, g_y, g_z
    )
    near_back, far_back, b_back, g_own = (
        left(near_left), right(far_right), over_y(b_y), over_z(g_ring)
    )
    near_opposite, far_opposite, b_yz, g_zy = experts(
        [near_opposite, far_opposite, b_yz, g_zy], *matrices
    )
    near_opposite, far_opposite, b_yz, g_y, near_back, far_back, b_back, g_own = together(
        near_opposite, far_opposite, b_yz, g_y, near_back, far_back, b_back, g_own
    )
    got = right(near_opposite), left(far_opposite), over_y(b_yz), over_z(g_y)
    near_right, far_left = add(near_right, got[0]), add(far_left, got[1])
    b_ring, g_zy = add(b_ring, b_back), add(g_zy, got[3])
    info, b_yz_back, near_right, far_left, b_ring, g_zy = together(
        info, got[2], near_right, far_left, b_ring, g_zy
    )
    *got, info = together(
        right(near_right), left(far_left), over_z(b_ring), over_y(g_zy), to_next_section(info)
    )

    near, far = (near, near_back, got[0]), (far, far_back, got[1])
    b_terms, g_terms = (b_z, b_yz_back, got[2]), (g_z, g_own, got[3])
    got = sums(
        [take(b_terms, 3, 4), take(g_terms, 2, 4)],
        [take(g_terms, 3, 4), take(b_terms, 2, 4)],
        [take(near, 0, 2)],
        [take(far, 1, 2)],
    )
    got = together(left(got[0]), right(got[1]), over_z(got[2]), over_y(got[3]))
    a1_terms = take(far, 0, 4), take(far, 1, 4)
    a2_terms = take(near, 2, 4), take(near, 3, 4)
    ends = sums(
        [take(b_terms, 1, 4) + take(got[:1], 0, 2)],
        [take(g_terms, 1, 4) + take(got[1:2], 0, 2)],
        [a1_terms[1] + take(got[2:3], 1, 2)],
        [a2_terms[0] + take(got[3:], 0, 2)],
    )
    ends = together(left(ends[0]), right(ends[1]), over_y(ends[2]), over_z(ends[3]))
    own, partner = sums(
        [
            a1_terms[0] + take(got[2:3], 0, 2) + take(ends[2:3], 0, 1),
            take(b_terms, 0, 4) + take(got[1:2], 1, 2) + take(ends[:1], 0, 1),
        ],
        [
            a2_terms[1] + take(got[3:], 1, 2) + take(ends[3:], 0, 1),
            take(g_terms, 0, 4) + take(got[:1], 1, 2) + take(ends[1:2], 0, 1),
        ],
    )

    own_done, other_done = to_owner(own), to_owner_across(partner)

    def contribution(position, weight, done):
        table = position[:, None] == jnp.arange(CAP, dtype=F32)[None]
        rows = jnp.dot(table.astype(BF16), done, preferred_element_type=F32)
        return weight[:, None] * rows

    mixed = contribution(info[0], info[2], own_done) + contribution(info[1], info[3], other_done)
    return mixed.astype(BF16)[None]


def solution(mesh):
    shape = (2, 2, 2, 2, 4, 2)
    fine = Mesh(mesh.devices.reshape(shape), ("zh", "core", "yh", "yl", "x", "zl"))
    section, ep = ("zh", "core"), ("yh", "yl", "x", "zl")
    rows = P(section, ep, None)
    columns = P(section, None, ep)
    return jax.shard_map(
        body,
        mesh=fine,
        in_specs=(rows, rows, rows, rows, columns, columns, rows),
        out_specs=rows,
        check_vma=False,
    )
```
